128 devices in a mesh: dp: 4 (over y_hi, core), tx: 4 (over x), ty: 8 (over y_lo, z).
Axes of the slice: x: 4, y: 4 (y_hi: 2, y_lo: 2; y = y_hi * 2 + y_lo), z: 4, core: 2. Of those that a mesh axis runs over, the one named last changes fastest.
Arguments:
- frames: bfloat16 [4, 12288, 1024], P('dp', ('tx', 'ty')), may hold values from -6 to 6
- first_conv_weight: bfloat16 [1024, 4096], replicated, may hold values from -0.125 to 0.125
- first_residual_projection: bfloat16 [1024, 1024], replicated, may hold values from -0.1875 to 0.1875
- second_conv_weight: bfloat16 [1024, 4096], replicated, may hold values from -0.125 to 0.125
- second_residual_projection: bfloat16 [1024, 1024], replicated, may hold values from -0.1875 to 0.1875
- out_grad: bfloat16 [4, 12288, 1024], P('dp', ('tx', 'ty')), may hold values from -6 to 6
Outputs:
- output_frames: bfloat16 [4, 12288, 1024], P('dp', ('tx', 'ty'))
- frame_grad: bfloat16 [4, 12288, 1024], P('dp', ('tx', 'ty'))
- conv_first_grad: float32 [1024, 4096], P('ty')
- proj_first_grad: float32 [1024, 1024], P('ty')
- conv_second_grad: float32 [1024, 4096], P('ty')
- proj_second_grad: float32 [1024, 1024], P('ty')
The draws below stay inside these ranges and needn't reach their ends.
All inputs are finite; a program needn't handle non-finite values.
Results may differ from the reference program's by a relative error of at most 0.023.
Values may be sent and summed in bfloat16 or wider, within the bound.
A program may use at most 128 MiB of HBM per device.

```python
import jax
import jax.numpy as jnp
from jax import lax

CHANNELS = 1024
FRAMES_DEV = 384
NEAR_DILATION = 64
FAR_DILATION = 3072
STREAM_LEN = 12288
STREAMS = 4


def raised(values, stream_key, source, target, shards_of, factor):
    def block_of(dim):
        return (jnp.arange(values.shape[dim]) // (values.shape[dim] // shards_of)).reshape((-1,) + (1,) * (values.ndim - 1 - dim))

    one_side = jax.random.permutation(stream_key, shards_of)[block_of(target)]
    far = (block_of(target) + shards_of // 2) % shards_of
    return jnp.where((block_of(source) == one_side) | (block_of(source) == far), factor * values, values)


def steps_of(key, dims, cuts, low, largest):
    gain = 1.0
    for dim, shards_of in cuts:
        heights = jax.random.uniform(jax.random.fold_in(jax.random.fold_in(key, 6), dim), (shards_of,), jnp.float32, low / len(cuts), largest / len(cuts))
        gain = gain * jnp.repeat(jnp.exp(heights), dims[dim] // shards_of).reshape((-1,) + (1,) * (len(dims) - 1 - dim))
    return gain


def bell_draw(rng, shape, width, reach, cuts=(), kind=jnp.bfloat16):
    level = steps_of(rng, shape, cuts, -0.22, 0.18) if cuts else 1.0
    array = jax.random.normal(rng, shape, jnp.float32) * width * level
    return jnp.minimum(jnp.maximum(array, -reach), reach).astype(kind)


def bell_draw_with(rng, extent, spread, bound, shards, heavy, held_as=jnp.bfloat16):
    array = spread * jax.random.normal(rng, extent, jnp.float32)
    if shards:
        array = array * steps_of(rng, extent, shards, -0.22, 0.18)
    return jnp.clip(raised(array, jax.random.fold_in(rng, 3), *heavy), -bound, bound).astype(held_as)


def setup_inputs(seed: int = 0) -> dict:
    seeds = jax.random.split(jax.random.key(seed), 7)
    return {
        "frames": bell_draw_with(seeds[0], (STREAMS, STREAM_LEN, CHANNELS), 1.0, 6.0, ((0, 4), (1, 32)), (1, 2, 32, 2.75)),
        "first_conv_weight": bell_draw(seeds[1], (CHANNELS, 4 * CHANNELS), (2 * CHANNELS) ** -0.5, 0.125),
        "first_residual_projection": bell_draw(seeds[2], (CHANNELS, CHANNELS), CHANNELS ** -0.5, 0.1875),
        "second_conv_weight": bell_draw(seeds[3], (CHANNELS, 4 * CHANNELS), (2 * CHANNELS) ** -0.5, 0.125),
        "second_residual_projection": bell_draw(seeds[4], (CHANNELS, CHANNELS), CHANNELS ** -0.5, 0.1875),
        "out_grad": bell_draw(seeds[5], (STREAMS, STREAM_LEN, CHANNELS), 1.0, 6.0, ((0, 4), (1, 32))),
    }


def delay_rows(value_rows, dilation):
    return jnp.concatenate([jnp.zeros((dilation, value_rows.shape[1]), value_rows.dtype), value_rows[:-dilation]], 0)


def advance_rows(value_rows, dilation):
    return jnp.concatenate([value_rows[dilation:], jnp.zeros((dilation, value_rows.shape[1]), value_rows.dtype)], 0)


def forward_layer_pass(input_frames, conv_weight, proj_weight, dilation):
    shifted = delay_rows(input_frames, dilation)
    pre = jnp.dot(shifted, conv_weight[:, :2 * CHANNELS], preferred_element_type=jnp.float32)
    pre = pre + jnp.dot(input_frames, conv_weight[:, 2 * CHANNELS:], preferred_element_type=jnp.float32)
    tanh_part = jnp.tanh(pre[:, :CHANNELS])
    gate_part = jax.nn.sigmoid(pre[:, CHANNELS:])
    gated = (tanh_part * gate_part).astype(jnp.bfloat16)
    output = (input_frames.astype(jnp.float32) + jnp.dot(gated, proj_weight, preferred_element_type=jnp.float32)).astype(jnp.bfloat16)
    return output, shifted, tanh_part, gate_part, gated


def backward_layer_pass(tanh_part, gate_part, grad_out, conv_weight, proj_weight, dilation):
    grad_gated = jnp.dot(grad_out, proj_weight.T, preferred_element_type=jnp.float32)
    grad_pre = jnp.concatenate([grad_gated * gate_part * (1.0 - tanh_part * tanh_part),
                                grad_gated * tanh_part * gate_part * (1.0 - gate_part)], 1).astype(jnp.bfloat16)
    tap_part = jnp.dot(grad_pre, conv_weight[:, :2 * CHANNELS].T, preferred_element_type=jnp.float32).astype(jnp.bfloat16)
    grad_in = grad_out.astype(jnp.float32) + jnp.dot(grad_pre, conv_weight[:, 2 * CHANNELS:].T, preferred_element_type=jnp.float32)
    grad_in = (grad_in + advance_rows(tap_part, dilation).astype(jnp.float32)).astype(jnp.bfloat16)
    return grad_in, grad_pre


def block_partials(shifted, input_frames, grad_pre, gated, grad_out):
    blocks = STREAM_LEN // FRAMES_DEV

    def split(value_rows):
        return value_rows.reshape(blocks, FRAMES_DEV, value_rows.shape[1])

    def advance(running, pieces):
        piece_shift, piece_in, piece_pre, piece_gated, piece_out = pieces
        term = jnp.concatenate([jnp.dot(piece_shift.T, piece_pre, preferred_element_type=jnp.float32),
                                jnp.dot(piece_in.T, piece_pre, preferred_element_type=jnp.float32),
                                jnp.dot(piece_gated.T, piece_out, preferred_element_type=jnp.float32)], 1)
        rounded = lax.optimization_barrier(term.astype(jnp.bfloat16))
        return running + rounded.astype(jnp.float32), None

    block_input = jnp.zeros((CHANNELS, 5 * CHANNELS), jnp.float32)
    running, unused = lax.scan(advance, block_input, (split(shifted), split(input_frames), split(grad_pre), split(gated), split(grad_out)))
    return running


def reference(frames, first_conv_weight, first_residual_projection, second_conv_weight, second_residual_projection, out_grad):
    def one_stream(stream_pair):
        block_input, output_gradient = stream_pair
        middle_activation, first_shifted_input, first_tanh_filter, first_gate, first_gated_value = forward_layer_pass(block_input, first_conv_weight, first_residual_projection, NEAR_DILATION)
        block_output, second_shifted_input, second_tanh_filter, second_gate, second_gated_value = forward_layer_pass(middle_activation, second_conv_weight, second_residual_projection, FAR_DILATION)
        middle_gradient, second_preactivation = backward_layer_pass(second_tanh_filter, second_gate, output_gradient, second_conv_weight, second_residual_projection, FAR_DILATION)
        input_gradient, first_preactivation = backward_layer_pass(first_tanh_filter, first_gate, middle_gradient, first_conv_weight, first_residual_projection, NEAR_DILATION)
        total_two = block_partials(second_shifted_input, middle_activation, second_preactivation, second_gated_value, output_gradient)
        total_one = block_partials(first_shifted_input, block_input, first_preactivation, first_gated_value, middle_gradient)
        return block_output, input_gradient, total_one, total_two

    finals, grads, totals_one, totals_two = lax.map(one_stream, (frames, out_grad))
    scale = float(STREAMS * STREAM_LEN) ** -0.5
    total_one = jnp.sum(totals_one, 0) * scale
    total_two = jnp.sum(totals_two, 0) * scale
    return (finals, grads, total_one[:, :4 * CHANNELS], total_one[:, 4 * CHANNELS:],
            total_two[:, :4 * CHANNELS], total_two[:, 4 * CHANNELS:])
```

```python
import jax
import jax.numpy as jnp
from jax import lax
from jax.experimental import pallas as pl
from jax.experimental.pallas import tpu as pltpu
from jax.sharding import PartitionSpec as P

NEAR_DILATION = 64


def shifted_2(value, axis, steps):
    count = lax.axis_size(axis)
    leading, last = (max(0, -steps), min(count, count - steps))
    return lax.ppermute(value, axis, [(source, source + steps) for source in range(leading, last)])


def mult_trans(left, right):
    return lax.dot_general(
        left, right, (((1,), (1,)), ((), ())), preferred_element_type=jnp.float32
    )


def contract_rows(left, right):
    return lax.dot_general(
        left, right, (((0,), (0,)), ((), ())), preferred_element_type=jnp.float32
    )


def fetch_near(input_frames):
    frame_rows = input_frames.shape[0]
    boundary_frames = shifted_2(input_frames[frame_rows - NEAR_DILATION :], ("tx", "ty"), 1)
    return jnp.concatenate([boundary_frames, input_frames[: frame_rows - NEAR_DILATION]], 0)


def fetch_far(input_frames):
    result = shifted_2(input_frames, ("tx", "ty"), lax.axis_size("ty"))
    return result


def back_near(value_rows):
    boundary_frames = shifted_2(value_rows[:NEAR_DILATION], ("tx", "ty"), -1)
    return jnp.concatenate([value_rows[NEAR_DILATION:], boundary_frames], 0)


def back_far(value_rows):
    result = shifted_2(value_rows, ("tx", "ty"), -lax.axis_size("ty"))
    return result


def causal_parts(input_frames, shifted, conv_weight, proj_weight):
    width = input_frames.shape[1]
    pre = jnp.dot(shifted, conv_weight[:, : 2 * width], preferred_element_type=jnp.float32)
    pre = pre + jnp.dot(
        input_frames, conv_weight[:, 2 * width :], preferred_element_type=jnp.float32
    )
    tanh_part = jnp.tanh(pre[:, :width])
    gate_part = jax.nn.sigmoid(pre[:, width:])
    gated = (tanh_part * gate_part).astype(jnp.bfloat16)
    output = (
        input_frames.astype(jnp.float32)
        + jnp.dot(gated, proj_weight, preferred_element_type=jnp.float32)
    ).astype(jnp.bfloat16)
    return (output, tanh_part, gate_part, gated)


def backward_layer_pass(tanh_part, gate_part, grad_out, conv_weight, proj_weight, send_back):
    width = grad_out.shape[1]
    grad_gated = mult_trans(grad_out, proj_weight)
    grad_pre = jnp.concatenate(
        [
            grad_gated * gate_part * (1.0 - tanh_part * tanh_part),
            grad_gated * tanh_part * gate_part * (1.0 - gate_part),
        ],
        1,
    ).astype(jnp.bfloat16)
    tap_weight = conv_weight[:, : 2 * width]
    tap_part = send_back(mult_trans(grad_pre, tap_weight).astype(jnp.bfloat16))
    grad_in = grad_out.astype(jnp.float32) + mult_trans(grad_pre, conv_weight[:, 2 * width :])
    grad_in = (grad_in + tap_part.astype(jnp.float32)).astype(jnp.bfloat16)
    return (grad_in, grad_pre)


MESH = pl.DeviceIdType.MESH
UNIT = 16
HALF = 2560
WIDTHS = ((4, 4, 3, 3, 3, 3), (3, 3, 4, 4, 3, 3))


def color_bounds(block):
    edges = [0]
    for width in WIDTHS[block]:
        edges.append(edges[-1] + 128 * width)
    return [(edges[i], edges[i + 1]) for i in range(6)]


def place():
    dp, tx, ty = (lax.axis_index(name) for name in ("dp", "tx", "ty"))
    y_hi, core = lax.div(dp, 2), lax.rem(dp, 2)
    y_lo, z = lax.div(ty, 4), lax.rem(ty, 4)
    zh, xh = lax.div(z, 2), lax.div(tx, 2)
    bits = (
        zh,
        lax.rem(zh + z, 2),
        y_hi,
        lax.rem(y_hi + y_lo, 2),
        xh,
        lax.rem(xh + tx, 2),
    )
    peers = (
        {"ty": y_lo * 4 + 3 - z},
        {"ty": y_lo * 4 + z + 1 - 2 * lax.rem(z, 2)},
        {"dp": (1 - y_hi) * 2 + core, "ty": (1 - y_lo) * 4 + z},
        {"ty": (1 - y_lo) * 4 + z},
        {"tx": 3 - tx},
        {"tx": tx + 1 - 2 * lax.rem(tx, 2)},
    )
    other_core = {"dp": y_hi * 2 + 1 - core}
    far_y = {"dp": (1 - y_hi) * 2 + core}
    return bits, core, peers, other_core, far_y


def order_of(color):
    return [(color + step) % 6 for step in range(6)]


def remote(source, target, send_sem, recv_sem, peer):
    return pltpu.make_async_remote_copy(
        src_ref=source,
        dst_ref=target,
        send_sem=send_sem,
        recv_sem=recv_sem,
        device_id=peer,
        device_id_type=MESH,
    )


def reduce_kernel(
    s2, x2, t2, p2, g2, s1, x1, t1, p1, g1, out,
    lhs_in, pre_in, grad_in, acc, got, full,
    ex_send, ex_recv, rs_send, rs_recv, ag_send, ag_recv, local_sem,
):
    bits, core, peers, other_core, far_y = place()
    blocks = ((s2, x2, t2, p2, g2), (s1, x1, t1, p1, g1))
    barrier = pltpu.get_barrier_semaphore()
    for peer in peers + (other_core, far_y):
        pl.semaphore_signal(barrier, inc=1, device_id=peer, device_id_type=MESH)
    pl.semaphore_wait(barrier, 8)

    def half(ref, which, width):
        return ref.at[:, pl.ds(pl.multiple_of(which * width, width), width)]

    exchange = []
    for b, (s, x, t, p, g) in enumerate(blocks):
        pairs = [
            (s, lhs_in.at[b, 0]),
            (x, lhs_in.at[b, 1]),
            (t, lhs_in.at[b, 2]),
            (half(p, 1 - core, 1024), pre_in.at[b]),
            (half(g, 1 - core, 512), grad_in.at[b]),
        ]
        copies = [
            remote(a, c, ex_send.at[b, i], ex_recv.at[b, i], other_core)
            for i, (a, c) in enumerate(pairs)
        ]
        for copy in copies:
            copy.start()
        exchange.append(copies)

    def weight_products(b):
        s, x, t, p, g = blocks[b]
        own_p, own_g = half(p, core, 1024), half(g, core, 512)
        bounds = color_bounds(b)

        def body(m, carry):
            start = pl.multiple_of(m * 256, 256)
            for part, own in enumerate((s, x, t)):
                left = jnp.concatenate(
                    [own[:, pl.ds(start, 256)], lhs_in[b, part, :, pl.ds(start, 256)]], 0
                )
                for piece in range(2 if part < 2 else 1):
                    if part < 2:
                        lo = piece * 512
                        right = jnp.concatenate(
                            [own_p[:, lo : lo + 512], pre_in[b, :, lo : lo + 512]], 0
                        )
                    else:
                        lo = 0
                        right = jnp.concatenate([own_g[...], grad_in[b]], 0)
                    product = contract_rows(left, right).astype(jnp.bfloat16)
                    first = part * 1024 + lo
                    for row in range(16):
                        ty = 2 * m + row // 8
                        y_lo, z = lax.div(ty, 4), lax.rem(ty, 4)
                        zh = lax.div(z, 2)
                        side = (row // 4) % 2
                        unit = (
                            zh,
                            lax.rem(zh + z, 2),
                            side,
                            lax.rem(side + y_lo, 2),
                            (row // 2) % 2,
                            row % 2,
                        )
                        for color, (begin, end) in enumerate(bounds):
                            begin, end = max(begin, first), min(end, first + 512)
                            if begin >= end:
                                continue
                            spot = 0
                            for step, dim in enumerate(order_of(color)):
                                spot = spot + unit[dim] * 2 ** (5 - step)
                            acc[b, spot, :, begin:end] = product[
                                row * 16 : row * 16 + 16, begin - first : end - first
                            ]
            return carry

        lax.fori_loop(0, 4, body, 0)

    def ranges(color, step):
        base = 0
        for earlier, dim in enumerate(order_of(color)[:step]):
            base = base + bits[dim] * 2 ** (5 - earlier)
        count = 2 ** (5 - step)
        mine = bits[order_of(color)[step]]
        return base + mine * count, base + (1 - mine) * count, count

    def reduce_copy(b, color, step):
        begin, end = color_bounds(b)[color]
        keep, give, count = ranges(color, step)
        spot = (b, pl.ds(give, count), slice(None), slice(begin, end))
        landing = (b, pl.ds(keep, count), slice(None), slice(begin, end))
        return remote(
            acc.at[spot], got.at[landing], rs_send.at[b, color, step],
            rs_recv.at[b, color, step], peers[order_of(color)[step]],
        )

    def arrival(b, color, step):
        begin, end = color_bounds(b)[color]
        keep, give, count = ranges(color, step)
        spot = (b, pl.ds(give, count), slice(None), slice(begin, end))
        return remote(
            acc.at[spot], got.at[spot], rs_send.at[b, color, step],
            rs_recv.at[b, color, step], peers[order_of(color)[step]],
        )

    def fold(b, color, step):
        begin, end = color_bounds(b)[color]
        keep, give, count = ranges(color, step)
        chunk = min(count, 4)

        def total(i):
            here = acc[b, pl.ds(keep + i * chunk, chunk), :, begin:end]
            there = got[b, pl.ds(give + i * chunk, chunk), :, begin:end]
            sum_ = here.astype(jnp.float32) + there.astype(jnp.float32)
            return sum_.astype(jnp.bfloat16)

        if step == 5:
            full[b, core, bits[2], bits[4], bits[5], :, begin:end] = total(0)[0]
            return

        def body(i, carry):
            acc[b, pl.ds(keep + i * chunk, chunk), :, begin:end] = total(i)
            return carry

        lax.fori_loop(0, count // chunk, body, 0)

    for b in range(2):
        for copy in exchange[b]:
            copy.wait_recv()
        weight_products(b)
        for color in range(6):
            reduce_copy(b, color, 0).start()
    for step in range(6):
        for b in range(2):
            for color in range(6):
                arrival(b, color, step).wait_recv()
                fold(b, color, step)
                if step < 5:
                    reduce_copy(b, color, step + 1).start()

    yh, xh, xq = bits[2], bits[4], bits[5]
    every = slice(None)

    def gather_copy(b, index, where, target):
        ref = full.at[(b, core) + where]
        return remote(ref, ref, ag_send.at[b, index], ag_recv.at[b, index], target)

    left, right = slice(0, HALF // 2), slice(HALF // 2, HALF)

    def first_copies(b):
        return [
            gather_copy(b, 1, (every, xh, xq, every, left), peers[5]),
            gather_copy(b, 2, (every, xh, xq, every, right), peers[4]),
        ]

    def second_copies(b):
        return [
            gather_copy(b, 3, (every, xh, every, every, left), peers[4]),
            gather_copy(b, 4, (every, every, xq, every, right), peers[5]),
        ]

    gathered = [[], []]
    for b in range(2):
        copy = gather_copy(b, 0, (yh, xh, xq), far_y)
        copy.start()
        gathered[b].append(copy)
    for b in range(2):
        gathered[b][0].wait_recv()
        for copy in first_copies(b):
            copy.start()
            gathered[b].append(copy)
    for b in range(2):
        gathered[b][1].wait_recv()
        gathered[b][2].wait_recv()
        for copy in second_copies(b):
            copy.start()
            gathered[b].append(copy)
    for b in range(2):
        gathered[b][3].wait_recv()
        gathered[b][4].wait_recv()
        ref = full.at[b, core]
        copy = remote(ref, ref, ag_send.at[b, 5], ag_recv.at[b, 5], other_core)
        copy.start()
        gathered[b].append(copy)
    for b in range(2):
        gathered[b][5].wait_recv()
        store = pltpu.make_async_copy(full.at[b], out.at[b], local_sem.at[b])
        store.start()
    for b in range(2):
        for copy in exchange[b] + gathered[b]:
            copy.wait_send()
        for color in range(6):
            for step in range(6):
                reduce_copy(b, color, step).wait_send()
        pltpu.make_async_copy(full.at[b], out.at[b], local_sem.at[b]).wait()


def weight_totals(*operands):
    vmem = pl.BlockSpec(memory_space=pltpu.VMEM)
    shape = (2, 2, 2, 2, 2, UNIT, HALF)
    return pl.pallas_call(
        reduce_kernel,
        out_shape=jax.ShapeDtypeStruct(shape, jnp.bfloat16),
        in_specs=[vmem] * 10,
        out_specs=pl.BlockSpec(memory_space=pl.ANY),
        scratch_shapes=[
            pltpu.VMEM((2, 3, 384, 1024), jnp.bfloat16),
            pltpu.VMEM((2, 384, 1024), jnp.bfloat16),
            pltpu.VMEM((2, 384, 512), jnp.bfloat16),
            pltpu.VMEM((2, 64, UNIT, HALF), jnp.bfloat16),
            pltpu.VMEM((2, 64, UNIT, HALF), jnp.bfloat16),
            pltpu.VMEM(shape, jnp.bfloat16),
            pltpu.SemaphoreType.DMA((2, 5)),
            pltpu.SemaphoreType.DMA((2, 5)),
            pltpu.SemaphoreType.DMA((2, 6, 6)),
            pltpu.SemaphoreType.DMA((2, 6, 6)),
            pltpu.SemaphoreType.DMA((2, 6)),
            pltpu.SemaphoreType.DMA((2, 6)),
            pltpu.SemaphoreType.DMA((2,)),
        ],
        compiler_params=pltpu.CompilerParams(
            collective_id=0, has_side_effects=True, vmem_limit_bytes=60 * 2**20
        ),
    )(*operands)


def scaled(total, rows):
    scale = float(
        lax.axis_size("dp") * lax.axis_size(("tx", "ty")) * rows
    ) ** (-0.5)
    total = total.reshape(2, 128, HALF)
    value = total.astype(jnp.float32) * scale
    conv = jnp.concatenate(
        [value[0, :, :1024], value[1, :, :1024], value[0, :, 1024:2048], value[1, :, 1024:2048]], 1
    )
    return conv, jnp.concatenate([value[0, :, 2048:], value[1, :, 2048:]], 1)


def shards(
    frames,
    first_conv_weight,
    first_residual_projection,
    second_conv_weight,
    second_residual_projection,
    out_grad,
):
    block_input = frames[0]
    output_gradient = out_grad[0]
    near_input = fetch_near(block_input)
    middle_activation, first_tanh_filter, first_gate, first_gated_value = causal_parts(
        block_input, near_input, first_conv_weight, first_residual_projection
    )
    far_input = fetch_far(middle_activation)
    block_output, second_tanh_filter, second_gate, second_gated_value = causal_parts(
        middle_activation, far_input, second_conv_weight, second_residual_projection
    )
    middle_gradient, second_preactivation = backward_layer_pass(
        second_tanh_filter,
        second_gate,
        output_gradient,
        second_conv_weight,
        second_residual_projection,
        back_far,
    )
    input_gradient, first_preactivation = backward_layer_pass(
        first_tanh_filter,
        first_gate,
        middle_gradient,
        first_conv_weight,
        first_residual_projection,
        back_near,
    )
    totals = weight_totals(
        far_input, middle_activation, second_gated_value, second_preactivation, output_gradient,
        near_input, block_input, first_gated_value, first_preactivation, middle_gradient,
    )
    conv_two_grad, proj_two_grad = scaled(totals[0], block_input.shape[0])
    conv_one_grad, proj_one_grad = scaled(totals[1], block_input.shape[0])
    return (
        block_output[None],
        input_gradient[None],
        conv_one_grad,
        proj_one_grad,
        conv_two_grad,
        proj_two_grad,
    )


def solution(mesh):
    return jax.shard_map(
        shards,
        mesh=mesh,
        in_specs=(P("dp", ("tx", "ty"), None), P(), P(), P(), P(), P("dp", ("tx", "ty"), None)),
        out_specs=(
            P("dp", ("tx", "ty"), None),
            P("dp", ("tx", "ty"), None),
            P("ty", None),
            P("ty", None),
            P("ty", None),
            P("ty", None),
        ),
        check_vma=False,
    )
```

```python
import jax
import jax.numpy as jnp
from jax import lax
from jax.experimental import pallas as pl
from jax.experimental.pallas import tpu as pltpu
from jax.sharding import PartitionSpec as P

NEAR = 64
ROWS = 384
WIDTH = 1024
CHUNKS = 2
CHUNK = ROWS // CHUNKS
TILE = 256

MESH = pl.DeviceIdType.MESH
UNIT = 16
HALF = 2560
WIDTHS = ((4, 4, 3, 3, 3, 3), (3, 3, 4, 4, 3, 3))


def color_bounds(block):
    edges = [0]
    for width in WIDTHS[block]:
        edges.append(edges[-1] + 128 * width)
    return [(edges[i], edges[i + 1]) for i in range(6)]


def place():
    dp, tx, ty = (lax.axis_index(name) for name in ("dp", "tx", "ty"))
    y_hi, core = lax.div(dp, 2), lax.rem(dp, 2)
    y_lo, z = lax.div(ty, 4), lax.rem(ty, 4)
    zh, xh = lax.div(z, 2), lax.div(tx, 2)
    bits = (
        zh,
        lax.rem(zh + z, 2),
        y_hi,
        lax.rem(y_hi + y_lo, 2),
        xh,
        lax.rem(xh + tx, 2),
    )
    peers = (
        {"ty": y_lo * 4 + 3 - z},
        {"ty": y_lo * 4 + z + 1 - 2 * lax.rem(z, 2)},
        {"dp": (1 - y_hi) * 2 + core, "ty": (1 - y_lo) * 4 + z},
        {"ty": (1 - y_lo) * 4 + z},
        {"tx": 3 - tx},
        {"tx": tx + 1 - 2 * lax.rem(tx, 2)},
    )
    other_core = {"dp": y_hi * 2 + 1 - core}
    far_y = {"dp": (1 - y_hi) * 2 + core}
    return bits, core, peers, other_core, far_y


def order_of(color):
    return [(color + step) % 6 for step in range(6)]


def remote(source, target, send_sem, recv_sem, peer):
    return pltpu.make_async_remote_copy(
        src_ref=source,
        dst_ref=target,
        send_sem=send_sem,
        recv_sem=recv_sem,
        device_id=peer,
        device_id_type=MESH,
    )


def dot_nn(left, right):
    return jnp.dot(left, right, preferred_element_type=jnp.float32)


def dot_nt(left, right):
    return lax.dot_general(
        left, right, (((1,), (1,)), ((), ())), preferred_element_type=jnp.float32
    )


def dot_tn(left, right):
    return lax.dot_general(
        left, right, (((0,), (0,)), ((), ())), preferred_element_type=jnp.float32
    )


def step_kernel(
    frames, conv_1, proj_1, conv_2, proj_2, out_grad,
    out_frames, frame_grad, totals,
    w1, w2, q1, q2, xs, mid, s2, t1, t2, g, gmid, gp1, gp2, slope_t, slope_g,
    tap_in, tap_out, near_tap, pre2, wide,
    xs_in, mid_in, s2_in, t1_in, t2_in, gp2_in, g_in, gp1_in, gm_in,
    acc2, got2, got1, full,
    ld_sem, near_send, near_recv, far_send, far_recv, ex_send, ex_recv,
    rs_send, rs_recv, ag_send, ag_recv, st_sem,
):
    bf16, f32 = jnp.bfloat16, jnp.float32
    bits, core, peers, other_core, far_y = place()
    tx, ty = lax.axis_index("tx"), lax.axis_index("ty")
    index = tx * 8 + ty
    after, before = lax.rem(index + 1, 32), lax.rem(index + 31, 32)
    next_peer = {"tx": lax.div(after, 8), "ty": lax.rem(after, 8)}
    prev_peer = {"tx": lax.div(before, 8), "ty": lax.rem(before, 8)}
    later_peer = {"tx": lax.rem(tx + 1, 4)}
    earlier_peer = {"tx": lax.rem(tx + 3, 4)}
    first_shard, last_shard = index == 0, index == 31

    def load(index, source, target):
        return pltpu.make_async_copy(source, target, ld_sem.at[index])

    def columns(start):
        return pl.ds(pl.multiple_of(start, TILE), TILE)

    def conv_loads(j):
        return [
            load(
                4 * j + part,
                conv_1.at[:, pl.ds(part * WIDTH + j * TILE, TILE)],
                w1.at[:, pl.ds(part * WIDTH + j * TILE, TILE)],
            )
            for part in range(4)
        ]

    loads = {"x": load(16, frames.at[0], xs.at[pl.ds(NEAR, ROWS), :])}
    loads["q1"] = load(17, proj_1, q1)
    loads["w2"] = load(18, conv_2, w2)
    loads["g"] = load(19, out_grad.at[0], g)
    loads["q2"] = load(20, proj_2, q2)
    loads["x"].start()
    for j in range(4):
        for copy in conv_loads(j):
            copy.start()
    for name in ("q1", "w2", "g", "q2"):
        loads[name].start()

    barrier = pltpu.get_barrier_semaphore()
    for peer in peers + (other_core, far_y, next_peer, prev_peer):
        pl.semaphore_signal(barrier, inc=1, device_id=peer, device_id_type=MESH)
    pl.semaphore_wait(barrier, 10)

    def half(ref, which, width):
        return ref.at[:, pl.ds(pl.multiple_of(which * width, width), width)]

    def half_rows(ref, which, width, rows):
        return ref.at[rows, pl.ds(pl.multiple_of(which * width, width), width)]

    def swap(item, part, source, target):
        return remote(
            source, target, ex_send.at[item, part], ex_recv.at[item, part], other_core
        )

    every = slice(None)
    top = pl.ds(0, NEAR)
    parts = [pl.ds(c * CHUNK, CHUNK) for c in range(CHUNKS)]
    swaps = {
        "x": [swap(0, 0, frames.at[0], xs_in.at[pl.ds(NEAR, ROWS), :])],
        "halo": [swap(1, 0, xs.at[top, :], xs_in.at[top, :])],
        "g": [swap(2, 0, half(out_grad.at[0], 1 - core, 512), g_in)],
    }
    for item, (name, source, target) in enumerate(
        (("t1", t1, t1_in), ("mid", mid, mid_in), ("s2", s2, s2_in), ("t2", t2, t2_in)), 3
    ):
        swaps[name] = [
            swap(item, c, source.at[rows, :], target.at[rows, :])
            for c, rows in enumerate(parts)
        ]
    for item, (name, source, target, width) in enumerate(
        (("gp2", gp2, gp2_in, 1024), ("gp1", gp1, gp1_in, 1024), ("gm", gmid, gm_in, 512)), 7
    ):
        swaps[name] = [
            swap(item, c, half_rows(source, 1 - core, width, rows), target.at[rows, :])
            for c, rows in enumerate(parts)
        ]

    near_forward = remote(
        frames.at[0, pl.ds(ROWS - NEAR, NEAR), :], xs.at[top, :],
        near_send.at[0], near_recv.at[0], next_peer,
    )
    near_back = remote(
        tap_out.at[top, :], near_tap, near_send.at[1], near_recv.at[1], prev_peer
    )
    far_forward = [
        remote(
            mid.at[rows, :], s2.at[rows, :], far_send.at[0, c], far_recv.at[0, c], later_peer
        )
        for c, rows in enumerate(parts)
    ]
    far_back = [
        remote(
            tap_out.at[rows, :], tap_in.at[rows, :],
            far_send.at[1, c], far_recv.at[1, c], earlier_peer,
        )
        for c, rows in enumerate(parts)
    ]

    near_forward.start()
    swaps["x"][0].start()
    swaps["g"][0].start()
    loads["x"].wait()
    near_forward.wait_recv()

    @pl.when(first_shard)
    def _():
        xs[0:NEAR, :] = jnp.zeros((NEAR, WIDTH), bf16)

    swaps["halo"][0].start()

    def tiles(count, body):
        def step(j, carry):
            body(j)
            return carry

        lax.fori_loop(0, count, step, 0)

    def first_forward(c):
        low = c * CHUNK
        rows = slice(low, low + CHUNK)
        moved = slice(NEAR + low, NEAR + low + CHUNK)

        def gate_tile(j):
            old, now = xs[rows, :], xs[moved, :]
            start = j * TILE
            a = dot_nn(old, w1[:, columns(start)]) + dot_nn(
                now, w1[:, columns(2 * WIDTH + start)]
            )
            v = dot_nn(old, w1[:, columns(WIDTH + start)]) + dot_nn(
                now, w1[:, columns(3 * WIDTH + start)]
            )
            th, gt = jnp.tanh(a), jax.nn.sigmoid(v)
            t1[rows, columns(start)] = (th * gt).astype(bf16)
            slope_t[rows, columns(start)] = (gt * (1.0 - th * th)).astype(bf16)
            slope_g[rows, columns(start)] = (th * gt * (1.0 - gt)).astype(bf16)

        if c == 0:
            for j in range(4):
                for copy in conv_loads(j):
                    copy.wait()
                gate_tile(j)
            loads["q1"].wait()
        else:
            tiles(4, gate_tile)
        swaps["t1"][c].start()

        def out_tile(j):
            value = dot_nn(t1[rows, :], q1[:, columns(j * TILE)])
            value = value + xs[moved, columns(j * TILE)].astype(f32)
            mid[rows, columns(j * TILE)] = value.astype(bf16)

        tiles(4, out_tile)
        far_forward[c].start()
        swaps["mid"][c].start()

    for c in range(CHUNKS):
        first_forward(c)

    loads["w2"].wait()

    def pre_tile(j):
        pre2[:, columns(j * TILE)] = dot_nn(mid[...], w2[:, columns(2 * WIDTH + j * TILE)])

    tiles(8, pre_tile)
    loads["g"].wait()
    loads["q2"].wait()

    def gated_grad_tile(j):
        wide[:, columns(j * TILE)] = dot_nt(g[...], q2[columns(j * TILE), :])

    tiles(4, gated_grad_tile)

    def second_block(c):
        low = c * CHUNK
        rows = slice(low, low + CHUNK)
        far_forward[c].wait_recv()

        @pl.when(tx == 0)
        def _():
            s2[rows, :] = jnp.zeros((CHUNK, WIDTH), bf16)

        swaps["s2"][c].start()

        def gate_tile(j):
            old = s2[rows, :]
            here, there = columns(j * TILE), columns(WIDTH + j * TILE)
            a = dot_nn(old, w2[:, here]) + pre2[rows, here]
            v = dot_nn(old, w2[:, there]) + pre2[rows, there]
            th, gt = jnp.tanh(a), jax.nn.sigmoid(v)
            t2[rows, here] = (th * gt).astype(bf16)
            grad = wide[rows, here] * gt
            gp2[rows, here] = (grad * (1.0 - th * th)).astype(bf16)
            gp2[rows, there] = (grad * th * (1.0 - gt)).astype(bf16)

        tiles(4, gate_tile)
        swaps["t2"][c].start()
        swaps["gp2"][c].start()

        def tap_tile(j):
            value = dot_nt(gp2[rows, :], w2[columns(j * TILE), 0 : 2 * WIDTH])
            tap_out[rows, columns(j * TILE)] = value.astype(bf16)

        tiles(4, tap_tile)
        far_back[c].start()

    for c in range(CHUNKS):
        second_block(c)

    def current_tile(j):
        value = dot_nt(gp2[...], w2[columns(j * TILE), 2 * WIDTH : 4 * WIDTH])
        wide[:, columns(j * TILE)] = value + g[:, columns(j * TILE)].astype(f32)

    tiles(4, current_tile)

    sums, arrivals = (acc2, w2), (got2, got1)

    def weight_products(b):
        if b == 0:
            lefts = ((s2, 0, s2_in), (mid, 0, mid_in), (t2, 0, t2_in))
            own_p, own_g = half(gp2, core, 1024), half(g, core, 512)
            pre_in, grad_in = gp2_in, g_in
        else:
            lefts = ((xs, 0, xs_in), (xs, NEAR, xs_in), (t1, 0, t1_in))
            own_p, own_g = half(gp1, core, 1024), half(gmid, core, 512)
            pre_in, grad_in = gp1_in, gm_in
        bounds = color_bounds(b)

        def product_tile(m):
            for part, (own, low, theirs) in enumerate(lefts):
                span = slice(low, low + ROWS)
                left = jnp.concatenate(
                    [own[span, columns(m * TILE)], theirs[span, columns(m * TILE)]], 0
                )
                for piece in range(2 if part < 2 else 1):
                    lo = piece * 512
                    if part < 2:
                        right = jnp.concatenate(
                            [own_p[:, lo : lo + 512], pre_in[:, lo : lo + 512]], 0
                        )
                    else:
                        right = jnp.concatenate([own_g[...], grad_in[...]], 0)
                    product = dot_tn(left, right).astype(bf16)
                    first = part * 1024 + lo
                    for row in range(16):
                        block = 2 * m + row // 8
                        y_lo, z = lax.div(block, 4), lax.rem(block, 4)
                        zh = lax.div(z, 2)
                        side = (row // 4) % 2
                        unit = (
                            zh,
                            lax.rem(zh + z, 2),
                            side,
                            lax.rem(side + y_lo, 2),
                            (row // 2) % 2,
                            row % 2,
                        )
                        for color, (begin, end) in enumerate(bounds):
                            begin, end = max(begin, first), min(end, first + 512)
                            if begin >= end:
                                continue
                            spot = 0
                            for step, dim in enumerate(order_of(color)):
                                spot = spot + unit[dim] * 2 ** (5 - step)
                            place_rows = pl.ds(pl.multiple_of(spot * UNIT, UNIT), UNIT)
                            sums[b][place_rows, begin:end] = product[
                                row * 16 : row * 16 + 16, begin - first : end - first
                            ]

        tiles(4, product_tile)

    def ranges(color, step):
        base = 0
        for earlier, dim in enumerate(order_of(color)[:step]):
            base = base + bits[dim] * 2 ** (5 - earlier)
        count = 2 ** (5 - step)
        mine = bits[order_of(color)[step]]
        return base + mine * count, base + (1 - mine) * count, count

    def units(start, count):
        return pl.ds(pl.multiple_of(start * UNIT, UNIT), count * UNIT)

    def reduce_copy(b, color, step, landing):
        begin, end = color_bounds(b)[color]
        keep, give, count = ranges(color, step)
        target = keep if landing else give
        return remote(
            sums[b].at[units(give, count), begin:end],
            arrivals[b].at[units(target, count), begin:end],
            rs_send.at[b, color, step], rs_recv.at[b, color, step],
            peers[order_of(color)[step]],
        )

    yh, xh, xq = bits[2], bits[4], bits[5]

    def fold(b, color, step):
        begin, end = color_bounds(b)[color]
        keep, give, count = ranges(color, step)
        chunk = min(count, 4)
        ours, theirs = sums[b], arrivals[b]

        def total(i):
            here = ours[units(keep + i * chunk, chunk), begin:end]
            there = theirs[units(give + i * chunk, chunk), begin:end]
            return (here.astype(f32) + there.astype(f32)).astype(bf16)

        if step == 5:
            full[b, core, yh, xh, xq, :, begin:end] = total(0)
            return

        def put(i):
            ours[units(keep + i * chunk, chunk), begin:end] = total(i)

        tiles(count // chunk, put)

    def advance(b, step):
        for color in range(6):
            reduce_copy(b, color, step, False).wait_recv()
            fold(b, color, step)
            if step < 5:
                reduce_copy(b, color, step + 1, True).start()

    def begin_reduce(b):
        for color in range(6):
            reduce_copy(b, color, 0, True).start()

    for name in ("mid", "s2", "t2", "gp2", "g"):
        for copy in swaps[name]:
            copy.wait_recv()
    weight_products(0)
    begin_reduce(0)

    def first_backward(c):
        low = c * CHUNK
        rows = slice(low, low + CHUNK)
        far_back[c].wait_recv()
        tap = tap_in[rows, :].astype(f32)
        total = wide[rows, :] + jnp.where(tx == 3, 0.0, tap)
        gmid[rows, :] = total.astype(bf16)
        swaps["gm"][c].start()

        def slope_tile(j):
            here, there = columns(j * TILE), columns(WIDTH + j * TILE)
            grad = dot_nt(gmid[rows, :], q1[here, :])
            gp1[rows, here] = (grad * slope_t[rows, here].astype(f32)).astype(bf16)
            gp1[rows, there] = (grad * slope_g[rows, here].astype(f32)).astype(bf16)

        tiles(4, slope_tile)
        swaps["gp1"][c].start()

    for c in range(CHUNKS):
        first_backward(c)
    advance(0, 0)
    for name in ("x", "halo", "t1", "gp1", "gm"):
        for copy in swaps[name]:
            copy.wait_recv()
    weight_products(1)
    begin_reduce(1)
    advance(0, 1)

    for copy in far_back:
        copy.wait_send()

    def first_tap_tile(j):
        value = dot_nt(gp1[...], w1[columns(j * TILE), 0 : 2 * WIDTH])
        tap_out[:, columns(j * TILE)] = value.astype(bf16)

    tiles(4, first_tap_tile)
    near_back.start()
    advance(0, 2)

    def first_current_tile(j):
        value = dot_nt(gp1[...], w1[columns(j * TILE), 2 * WIDTH : 4 * WIDTH])
        pre2[:, columns(j * TILE)] = value + gmid[:, columns(j * TILE)].astype(f32)

    tiles(4, first_current_tile)
    advance(0, 3)
    for copy in far_forward + swaps["mid"]:
        copy.wait_send()

    def second_out_tile(j):
        value = dot_nn(t2[...], q2[:, columns(j * TILE)])
        mid[:, columns(j * TILE)] = (value + mid[:, columns(j * TILE)].astype(f32)).astype(bf16)

    tiles(4, second_out_tile)
    store_out = pltpu.make_async_copy(mid, out_frames.at[0], st_sem.at[0])
    store_out.start()
    advance(1, 0)
    advance(0, 4)
    near_back.wait_recv()
    for copy in swaps["gm"]:
        copy.wait_send()
    body_rows = ROWS - NEAR
    gmid[0:body_rows, :] = (
        pre2[0:body_rows, 0:WIDTH] + tap_out[NEAR:ROWS, :].astype(f32)
    ).astype(bf16)
    edge = jnp.where(last_shard, 0.0, near_tap[...].astype(f32))
    gmid[body_rows:ROWS, :] = (pre2[body_rows:ROWS, 0:WIDTH] + edge).astype(bf16)
    store_grad = pltpu.make_async_copy(gmid, frame_grad.at[0], st_sem.at[1])
    store_grad.start()

    left, right = slice(0, HALF // 2), slice(HALF // 2, HALF)

    def gather_copy(b, index, where, target):
        ref = full.at[(b, core) + where]
        return remote(ref, ref, ag_send.at[b, index], ag_recv.at[b, index], target)

    def gather(b, index):
        if index == 0:
            return gather_copy(b, 0, (yh, xh, xq), far_y)
        if index == 1:
            return gather_copy(b, 1, (every, xh, xq, every, left), peers[5])
        if index == 2:
            return gather_copy(b, 2, (every, xh, xq, every, right), peers[4])
        if index == 3:
            return gather_copy(b, 3, (every, xh, every, every, left), peers[4])
        if index == 4:
            return gather_copy(b, 4, (every, every, xq, every, right), peers[5])
        return gather_copy(b, 5, (), other_core)

    def gather_stage(b, stage):
        waits = ((), (0,), (1, 2), (3, 4), (5,))[stage]
        starts = ((0,), (1, 2), (3, 4), (5,), ())[stage]
        for index in waits:
            gather(b, index).wait_recv()
        for index in starts:
            gather(b, index).start()
        if stage == 4:
            pltpu.make_async_copy(full.at[b], totals.at[b], st_sem.at[2 + b]).start()

    advance(1, 1)
    advance(0, 5)
    gather_stage(0, 0)
    advance(1, 2)
    gather_stage(0, 1)
    advance(1, 3)
    gather_stage(0, 2)
    advance(1, 4)
    gather_stage(0, 3)
    advance(1, 5)
    gather_stage(1, 0)
    gather_stage(0, 4)
    for stage in range(1, 5):
        gather_stage(1, stage)

    near_forward.wait_send()
    near_back.wait_send()
    for name, copies in swaps.items():
        if name not in ("mid", "gm"):
            for copy in copies:
                copy.wait_send()
    for b in range(2):
        for index in range(6):
            gather(b, index).wait_send()
        for color in range(6):
            for step in range(6):
                reduce_copy(b, color, step, True).wait_send()
        pltpu.make_async_copy(full.at[b], totals.at[b], st_sem.at[2 + b]).wait()
    store_out.wait()
    store_grad.wait()


def whole_step(*operands):
    anywhere = pl.BlockSpec(memory_space=pl.ANY)
    bf16, f32 = jnp.bfloat16, jnp.float32
    frame_shape = jax.ShapeDtypeStruct((1, ROWS, WIDTH), bf16)
    totals_shape = (2, 2, 2, 2, 2, UNIT, HALF)
    frame = pltpu.VMEM((ROWS, WIDTH), bf16)
    double = pltpu.VMEM((ROWS, 2 * WIDTH), bf16)
    narrow = pltpu.VMEM((ROWS, WIDTH // 2), bf16)
    weight = pltpu.VMEM((WIDTH, 4 * WIDTH), bf16)
    square = pltpu.VMEM((WIDTH, WIDTH), bf16)
    padded = pltpu.VMEM((ROWS + NEAR, WIDTH), bf16)
    share = pltpu.VMEM((WIDTH, HALF), bf16)
    dma = pltpu.SemaphoreType.DMA
    return pl.pallas_call(
        step_kernel,
        out_shape=[frame_shape, frame_shape, jax.ShapeDtypeStruct(totals_shape, bf16)],
        in_specs=[anywhere] * 6,
        out_specs=[anywhere] * 3,
        scratch_shapes=[
            weight, weight, square, square,
            padded, frame, frame, frame, frame, frame, frame,
            double, double, frame, frame,
            frame, frame, pltpu.VMEM((NEAR, WIDTH), bf16),
            pltpu.VMEM((ROWS, 2 * WIDTH), f32), pltpu.VMEM((ROWS, WIDTH), f32),
            padded, frame, frame, frame, frame, frame, narrow, frame, narrow,
            share, share, share, pltpu.VMEM(totals_shape, bf16),
            dma((21,)), dma((2,)), dma((2,)), dma((2, CHUNKS)), dma((2, CHUNKS)),
            dma((10, CHUNKS)), dma((10, CHUNKS)),
            dma((2, 6, 6)), dma((2, 6, 6)), dma((2, 6)), dma((2, 6)), dma((4,)),
        ],
        compiler_params=pltpu.CompilerParams(
            collective_id=0, has_side_effects=True, vmem_limit_bytes=67043328
        ),
    )(*operands)


def scaled(total, rows):
    scale = float(
        lax.axis_size("dp") * lax.axis_size(("tx", "ty")) * rows
    ) ** (-0.5)
    total = total.reshape(2, 128, HALF)
    value = total.astype(jnp.float32) * scale
    conv = jnp.concatenate(
        [value[0, :, :1024], value[1, :, :1024], value[0, :, 1024:2048], value[1, :, 1024:2048]], 1
    )
    return conv, jnp.concatenate([value[0, :, 2048:], value[1, :, 2048:]], 1)


def shards(*operands):
    block_output, input_gradient, totals = whole_step(*operands)
    conv_two_grad, proj_two_grad = scaled(totals[0], ROWS)
    conv_one_grad, proj_one_grad = scaled(totals[1], ROWS)
    return (
        block_output,
        input_gradient,
        conv_one_grad,
        proj_one_grad,
        conv_two_grad,
        proj_two_grad,
    )


def solution(mesh):
    return jax.shard_map(
        shards,
        mesh=mesh,
        in_specs=(P("dp", ("tx", "ty"), None), P(), P(), P(), P(), P("dp", ("tx", "ty"), None)),
        out_specs=(
            P("dp", ("tx", "ty"), None),
            P("dp", ("tx", "ty"), None),
            P("ty", None),
            P("ty", None),
            P("ty", None),
            P("ty", None),
        ),
        check_vma=False,
    )
```

```python
import jax
import jax.numpy as jnp
from jax import lax
from jax.experimental import pallas as pl
from jax.experimental.pallas import tpu as pltpu
from jax.sharding import PartitionSpec as P

NEAR = 64
ROWS = 384
WIDTH = 1024
CHUNKS = 2
CHUNK = ROWS // CHUNKS
TILE = 256

MESH = pl.DeviceIdType.MESH
UNIT = 16
HALF = 2560
SLABS = 10
ORDERS = (
    (
        (0, 2, 1, 4, 3, 5),
        (1, 5, 2, 3, 0, 4),
        (2, 0, 3, 5, 4, 1),
        (3, 1, 0, 2, 4, 5),
        (4, 5, 3, 1, 2, 0),
        (5, 3, 0, 2, 1, 4),
        (0, 3, 4, 5, 1, 2),
        (1, 5, 4, 2, 3, 0),
        (2, 4, 1, 5, 0, 3),
        (4, 3, 5, 0, 2, 1),
    ),
    (
        (1, 3, 5, 2, 4, 0),
        (0, 5, 3, 4, 2, 1),
        (3, 0, 1, 4, 5, 2),
        (2, 4, 0, 3, 1, 5),
        (5, 2, 1, 3, 0, 4),
        (4, 2, 5, 1, 0, 3),
        (1, 4, 3, 2, 0, 5),
        (0, 1, 2, 4, 5, 3),
        (3, 2, 0, 4, 1, 5),
        (5, 4, 2, 0, 1, 3),
    ),
)


def place():
    dp, tx, ty = (lax.axis_index(name) for name in ("dp", "tx", "ty"))
    y_hi, core = lax.div(dp, 2), lax.rem(dp, 2)
    y_lo, z = lax.div(ty, 4), lax.rem(ty, 4)
    zh, xh = lax.div(z, 2), lax.div(tx, 2)
    bits = (
        zh,
        lax.rem(zh + z, 2),
        y_hi,
        lax.rem(y_hi + y_lo, 2),
        xh,
        lax.rem(xh + tx, 2),
    )
    peers = (
        {"ty": y_lo * 4 + 3 - z},
        {"ty": y_lo * 4 + z + 1 - 2 * lax.rem(z, 2)},
        {"dp": (1 - y_hi) * 2 + core, "ty": (1 - y_lo) * 4 + z},
        {"ty": (1 - y_lo) * 4 + z},
        {"tx": 3 - tx},
        {"tx": tx + 1 - 2 * lax.rem(tx, 2)},
    )
    other_core = {"dp": y_hi * 2 + 1 - core}
    far_y = {"dp": (1 - y_hi) * 2 + core}
    return bits, core, peers, other_core, far_y


def remote(source, target, send_sem, recv_sem, peer):
    return pltpu.make_async_remote_copy(
        src_ref=source,
        dst_ref=target,
        send_sem=send_sem,
        recv_sem=recv_sem,
        device_id=peer,
        device_id_type=MESH,
    )


def dot_nn(left, right):
    return jnp.dot(left, right, preferred_element_type=jnp.float32)


def dot_nt(left, right):
    return lax.dot_general(
        left, right, (((1,), (1,)), ((), ())), preferred_element_type=jnp.float32
    )


def dot_tn(left, right):
    return lax.dot_general(
        left, right, (((0,), (0,)), ((), ())), preferred_element_type=jnp.float32
    )


def step_kernel(
    frames, conv_1, proj_1, conv_2, proj_2, out_grad,
    out_frames, frame_grad, conv_total_2, proj_total_2, conv_total_1, proj_total_1,
    w1, w2, q1, q2, xs, mid, s2, t1, t2, g, gmid, gp1, gp2, slope_t, slope_g,
    tap_in, tap_out, near_tap, pre2, wide,
    xs_in, mid_in, s2_in, t1_in, t2_in, gp2_in, g_in, gp1_in, gm_in,
    acc2, got2, got1, full,
    ld_sem, near_send, near_recv, far_send, far_recv, ex_send, ex_recv,
    rs_send, rs_recv, ag_send, ag_recv, st_sem,
):
    bf16, f32 = jnp.bfloat16, jnp.float32
    bits, core, peers, other_core, far_y = place()
    tx, ty = lax.axis_index("tx"), lax.axis_index("ty")
    index = tx * 8 + ty
    after, before = lax.rem(index + 1, 32), lax.rem(index + 31, 32)
    next_peer = {"tx": lax.div(after, 8), "ty": lax.rem(after, 8)}
    prev_peer = {"tx": lax.div(before, 8), "ty": lax.rem(before, 8)}
    later_peer = {"tx": lax.rem(tx + 1, 4)}
    earlier_peer = {"tx": lax.rem(tx + 3, 4)}
    first_shard, last_shard = index == 0, index == 31

    def load(index, source, target):
        return pltpu.make_async_copy(source, target, ld_sem.at[index])

    def columns(start):
        return pl.ds(pl.multiple_of(start, TILE), TILE)

    def conv_loads(j):
        return [
            load(
                4 * j + part,
                conv_1.at[:, pl.ds(part * WIDTH + j * TILE, TILE)],
                w1.at[:, pl.ds(part * WIDTH + j * TILE, TILE)],
            )
            for part in range(4)
        ]

    loads = {"x": load(16, frames.at[0], xs.at[pl.ds(NEAR, ROWS), :])}
    loads["q1"] = load(17, proj_1, q1)
    loads["w2"] = load(18, conv_2, w2)
    loads["g"] = load(19, out_grad.at[0], g)
    loads["q2"] = load(20, proj_2, q2)
    loads["x"].start()
    for j in range(4):
        for copy in conv_loads(j):
            copy.start()
    loads["q1"].start()

    barrier = pltpu.get_barrier_semaphore()
    for peer in peers + (other_core, far_y, next_peer, prev_peer):
        pl.semaphore_signal(barrier, inc=1, device_id=peer, device_id_type=MESH)
    pl.semaphore_wait(barrier, 10)

    def half(ref, which, width):
        return ref.at[:, pl.ds(pl.multiple_of(which * width, width), width)]

    def half_rows(ref, which, width, rows):
        return ref.at[rows, pl.ds(pl.multiple_of(which * width, width), width)]

    def swap(item, part, source, target):
        return remote(
            source, target, ex_send.at[item, part], ex_recv.at[item, part], other_core
        )

    every = slice(None)
    top = pl.ds(0, NEAR)
    parts = [pl.ds(c * CHUNK, CHUNK) for c in range(CHUNKS)]
    swaps = {
        "x": [swap(0, 0, frames.at[0], xs_in.at[pl.ds(NEAR, ROWS), :])],
        "halo": [swap(1, 0, xs.at[top, :], xs_in.at[top, :])],
        "g": [swap(2, 0, half(out_grad.at[0], 1 - core, 512), g_in)],
    }
    for item, (name, source, target) in enumerate(
        (("t1", t1, t1_in), ("mid", mid, mid_in), ("s2", s2, s2_in), ("t2", t2, t2_in)), 3
    ):
        swaps[name] = [
            swap(item, c, source.at[rows, :], target.at[rows, :])
            for c, rows in enumerate(parts)
        ]
    for item, (name, source, target, width) in enumerate(
        (("gp2", gp2, gp2_in, 1024), ("gp1", gp1, gp1_in, 1024), ("gm", gmid, gm_in, 512)), 7
    ):
        swaps[name] = [
            swap(item, c, half_rows(source, 1 - core, width, rows), target.at[rows, :])
            for c, rows in enumerate(parts)
        ]

    near_forward = remote(
        frames.at[0, pl.ds(ROWS - NEAR, NEAR), :], xs.at[top, :],
        near_send.at[0], near_recv.at[0], next_peer,
    )
    near_back = remote(
        tap_out.at[top, :], near_tap, near_send.at[1], near_recv.at[1], prev_peer
    )
    far_forward = [
        remote(
            mid.at[rows, :], s2.at[rows, :], far_send.at[0, c], far_recv.at[0, c], later_peer
        )
        for c, rows in enumerate(parts)
    ]
    far_back = [
        remote(
            tap_out.at[rows, :], tap_in.at[rows, :],
            far_send.at[1, c], far_recv.at[1, c], earlier_peer,
        )
        for c, rows in enumerate(parts)
    ]

    near_forward.start()
    swaps["x"][0].start()
    swaps["g"][0].start()
    loads["x"].wait()
    near_forward.wait_recv()

    @pl.when(first_shard)
    def _():
        xs[0:NEAR, :] = jnp.zeros((NEAR, WIDTH), bf16)

    swaps["halo"][0].start()

    def tiles(count, body):
        def step(j, carry):
            body(j)
            return carry

        lax.fori_loop(0, count, step, 0)

    def first_forward(c):
        low = c * CHUNK
        rows = slice(low, low + CHUNK)
        moved = slice(NEAR + low, NEAR + low + CHUNK)

        def gate_tile(j):
            old, now = xs[rows, :], xs[moved, :]
            start = j * TILE
            a = dot_nn(old, w1[:, columns(start)]) + dot_nn(
                now, w1[:, columns(2 * WIDTH + start)]
            )
            v = dot_nn(old, w1[:, columns(WIDTH + start)]) + dot_nn(
                now, w1[:, columns(3 * WIDTH + start)]
            )
            th, gt = jnp.tanh(a), jax.nn.sigmoid(v)
            t1[rows, columns(start)] = (th * gt).astype(bf16)
            slope_t[rows, columns(start)] = (gt * (1.0 - th * th)).astype(bf16)
            slope_g[rows, columns(start)] = (th * gt * (1.0 - gt)).astype(bf16)

        if c == 0:
            for j in range(4):
                for copy in conv_loads(j):
                    copy.wait()
                gate_tile(j)
                if j == 0:
                    for name in ("w2", "g", "q2"):
                        loads[name].start()
            loads["q1"].wait()
        else:
            tiles(4, gate_tile)
        swaps["t1"][c].start()

        def out_tile(j):
            value = dot_nn(t1[rows, :], q1[:, columns(j * TILE)])
            value = value + xs[moved, columns(j * TILE)].astype(f32)
            mid[rows, columns(j * TILE)] = value.astype(bf16)

        tiles(4, out_tile)
        far_forward[c].start()
        swaps["mid"][c].start()

    for c in range(CHUNKS):
        first_forward(c)

    loads["w2"].wait()

    def pre_tile(j):
        pre2[:, columns(j * TILE)] = dot_nn(mid[...], w2[:, columns(2 * WIDTH + j * TILE)])

    tiles(8, pre_tile)
    loads["g"].wait()
    loads["q2"].wait()

    def gated_grad_tile(j):
        wide[:, columns(j * TILE)] = dot_nt(g[...], q2[columns(j * TILE), :])

    tiles(4, gated_grad_tile)

    def second_block(c):
        low = c * CHUNK
        rows = slice(low, low + CHUNK)
        far_forward[c].wait_recv()

        @pl.when(tx == 0)
        def _():
            s2[rows, :] = jnp.zeros((CHUNK, WIDTH), bf16)

        swaps["s2"][c].start()

        def gate_tile(j):
            old = s2[rows, :]
            here, there = columns(j * TILE), columns(WIDTH + j * TILE)
            a = dot_nn(old, w2[:, here]) + pre2[rows, here]
            v = dot_nn(old, w2[:, there]) + pre2[rows, there]
            th, gt = jnp.tanh(a), jax.nn.sigmoid(v)
            t2[rows, here] = (th * gt).astype(bf16)
            grad = wide[rows, here] * gt
            gp2[rows, here] = (grad * (1.0 - th * th)).astype(bf16)
            gp2[rows, there] = (grad * th * (1.0 - gt)).astype(bf16)

        tiles(4, gate_tile)
        swaps["t2"][c].start()
        swaps["gp2"][c].start()

        def tap_tile(j):
            value = dot_nt(gp2[rows, :], w2[columns(j * TILE), 0 : 2 * WIDTH])
            tap_out[rows, columns(j * TILE)] = value.astype(bf16)

        tiles(4, tap_tile)
        far_back[c].start()

    for c in range(CHUNKS):
        second_block(c)

    def current_tile(j):
        value = dot_nt(gp2[...], w2[columns(j * TILE), 2 * WIDTH : 4 * WIDTH])
        wide[:, columns(j * TILE)] = value + g[:, columns(j * TILE)].astype(f32)

    tiles(4, current_tile)

    def units(start, count):
        return pl.ds(pl.multiple_of(start * UNIT, UNIT), count * UNIT)

    def ours(b, slab, rows):
        if b == 0:
            return acc2.at[slab, rows, :]
        return w2.at[rows, slab * TILE : slab * TILE + TILE]

    def theirs(b, slab, rows):
        return (got2, got1)[b].at[slab, rows, :]

    def weight_products(b):
        if b == 0:
            lefts = ((s2, 0, s2_in), (mid, 0, mid_in), (t2, 0, t2_in))
            own_p, own_g = half(gp2, core, 1024), half(g, core, 512)
            pre_in, grad_in = gp2_in, g_in
        else:
            lefts = ((xs, 0, xs_in), (xs, NEAR, xs_in), (t1, 0, t1_in))
            own_p, own_g = half(gp1, core, 1024), half(gmid, core, 512)
            pre_in, grad_in = gp1_in, gm_in
        def product_tile(m):
            for part, (own, low, theirs) in enumerate(lefts):
                span = slice(low, low + ROWS)
                left = jnp.concatenate(
                    [own[span, columns(m * TILE)], theirs[span, columns(m * TILE)]], 0
                )
                for piece in range(2 if part < 2 else 1):
                    lo = piece * 512
                    if part < 2:
                        right = jnp.concatenate(
                            [own_p[:, lo : lo + 512], pre_in[:, lo : lo + 512]], 0
                        )
                    else:
                        right = jnp.concatenate([own_g[...], grad_in[...]], 0)
                    product = dot_tn(left, right).astype(bf16)
                    first = part * 1024 + lo
                    for row in range(16):
                        block = 2 * m + row // 8
                        y_lo, z = lax.div(block, 4), lax.rem(block, 4)
                        zh = lax.div(z, 2)
                        side = (row // 4) % 2
                        unit = (
                            zh,
                            lax.rem(zh + z, 2),
                            side,
                            lax.rem(side + y_lo, 2),
                            (row // 2) % 2,
                            row % 2,
                        )
                        for local in range(2):
                            slab = first // TILE + local
                            spot = 0
                            for step, dim in enumerate(ORDERS[b][slab]):
                                spot = spot + unit[dim] * 2 ** (5 - step)
                            ours(b, slab, units(spot, 1))[...] = product[
                                row * 16 : row * 16 + 16, local * TILE : local * TILE + TILE
                            ]

        tiles(4, product_tile)

    def ranges(b, slab, step):
        base = 0
        for earlier, dim in enumerate(ORDERS[b][slab][:step]):
            base = base + bits[dim] * 2 ** (5 - earlier)
        count = 2 ** (5 - step)
        mine = bits[ORDERS[b][slab][step]]
        return base + mine * count, base + (1 - mine) * count, count

    def reduce_copy(b, slab, step, landing):
        keep, give, count = ranges(b, slab, step)
        return remote(
            ours(b, slab, units(give, count)),
            theirs(b, slab, units(keep if landing else give, count)),
            rs_send.at[b, slab, step], rs_recv.at[b, slab, step],
            peers[ORDERS[b][slab][step]],
        )

    yh, xh, xq = bits[2], bits[4], bits[5]

    def fold(b, slab, step):
        keep, give, count = ranges(b, slab, step)
        chunk = min(count, 16)

        def total(i):
            here = ours(b, slab, units(keep + i * chunk, chunk))[...]
            return here + theirs(b, slab, units(give + i * chunk, chunk))[...]

        if step == 5:
            full[b, core, yh, xh, xq, :, slab * TILE : slab * TILE + TILE] = total(0)
            return
        for i in range(count // chunk):
            ours(b, slab, units(keep + i * chunk, chunk))[...] = total(i)

    def advance(b, step):
        for slab in range(SLABS):
            reduce_copy(b, slab, step, False).wait_recv()
            fold(b, slab, step)
            if step < 5:
                reduce_copy(b, slab, step + 1, True).start()

    def begin_reduce(b):
        for slab in range(SLABS):
            reduce_copy(b, slab, 0, True).start()

    for name in ("mid", "s2", "t2", "gp2", "g"):
        for copy in swaps[name]:
            copy.wait_recv()
    weight_products(0)
    begin_reduce(0)

    def first_backward(c):
        low = c * CHUNK
        rows = slice(low, low + CHUNK)
        far_back[c].wait_recv()
        tap = tap_in[rows, :].astype(f32)
        total = wide[rows, :] + jnp.where(tx == 3, 0.0, tap)
        gmid[rows, :] = total.astype(bf16)
        swaps["gm"][c].start()

        def slope_tile(j):
            here, there = columns(j * TILE), columns(WIDTH + j * TILE)
            grad = dot_nt(gmid[rows, :], q1[here, :])
            gp1[rows, here] = (grad * slope_t[rows, here].astype(f32)).astype(bf16)
            gp1[rows, there] = (grad * slope_g[rows, here].astype(f32)).astype(bf16)

        tiles(4, slope_tile)
        swaps["gp1"][c].start()

    for c in range(CHUNKS):
        first_backward(c)
    for name in ("x", "halo", "t1", "gp1", "gm"):
        for copy in swaps[name]:
            copy.wait_recv()
    weight_products(1)
    begin_reduce(1)
    advance(0, 0)

    for copy in far_back:
        copy.wait_send()

    def first_tap_tile(j):
        value = dot_nt(gp1[...], w1[columns(j * TILE), 0 : 2 * WIDTH])
        tap_out[:, columns(j * TILE)] = value.astype(bf16)

    tiles(4, first_tap_tile)
    near_back.start()
    advance(0, 1)

    def first_current_tile(j):
        value = dot_nt(gp1[...], w1[columns(j * TILE), 2 * WIDTH : 4 * WIDTH])
        pre2[:, columns(j * TILE)] = value + gmid[:, columns(j * TILE)].astype(f32)

    tiles(4, first_current_tile)
    for copy in far_forward + swaps["mid"]:
        copy.wait_send()

    def second_out_tile(j):
        value = dot_nn(t2[...], q2[:, columns(j * TILE)])
        mid[:, columns(j * TILE)] = (value + mid[:, columns(j * TILE)].astype(f32)).astype(bf16)

    tiles(4, second_out_tile)
    store_out = pltpu.make_async_copy(mid, out_frames.at[0], st_sem.at[0])
    store_out.start()
    advance(1, 0)
    advance(0, 2)
    near_back.wait_recv()
    for copy in swaps["gm"]:
        copy.wait_send()
    body_rows = ROWS - NEAR
    gmid[0:body_rows, :] = (
        pre2[0:body_rows, 0:WIDTH] + tap_out[NEAR:ROWS, :].astype(f32)
    ).astype(bf16)
    edge = jnp.where(last_shard, 0.0, near_tap[...].astype(f32))
    gmid[body_rows:ROWS, :] = (pre2[body_rows:ROWS, 0:WIDTH] + edge).astype(bf16)
    store_grad = pltpu.make_async_copy(gmid, frame_grad.at[0], st_sem.at[1])
    store_grad.start()

    left, right = slice(0, HALF // 2), slice(HALF // 2, HALF)

    def gather_copy(b, index, where, target):
        ref = full.at[(b, core) + where]
        return remote(ref, ref, ag_send.at[b, index], ag_recv.at[b, index], target)

    places = (
        ((yh, xh, xq), far_y),
        ((every, xh, xq, every, left), peers[5]),
        ((every, xh, xq, every, right), peers[4]),
        ((every, xh, every, every, left), peers[4]),
        ((every, every, xq, every, right), peers[5]),
        ((every, xh, xq), other_core),
        ((every, xh, 1 - xq, every, left), other_core),
        ((every, 1 - xh, xq, every, right), other_core),
        ((every, 1 - xh, every, every, left), other_core),
        ((every, every, 1 - xq, every, right), other_core),
    )

    def gather(b, index):
        return gather_copy(b, index, *places[index])

    def stores(b):
        conv, proj = ((conv_total_2, proj_total_2), (conv_total_1, proj_total_1))[b]
        copies = []
        for k in range(2):
            moves = (
                (conv, k * 1024, 0, 1024),
                (conv, 2048 + k * 1024, 1024, 1024),
                (proj, k * 512, 2048, 512),
            )
            for target, to, start, width in moves:
                copies.append(
                    pltpu.make_async_copy(
                        full.at[b, k, :, :, :, :, start : start + width],
                        target.at[:, :, :, :, to : to + width],
                        st_sem.at[2 + b * 6 + len(copies)],
                    )
                )
        return copies

    def gather_stage(b, stage):
        waits = ((), (0,), (1, 2), (3, 4), (5, 6, 7, 8, 9))[stage]
        starts = ((0,), (1, 2, 5), (3, 4, 6, 7), (8, 9), ())[stage]
        for index in waits:
            gather(b, index).wait_recv()
        for index in starts:
            gather(b, index).start()
        if stage == 4:
            for copy in stores(b):
                copy.start()

    advance(1, 1)
    advance(0, 3)
    advance(1, 2)
    advance(0, 4)
    advance(1, 3)
    advance(0, 5)
    gather_stage(0, 0)
    advance(1, 4)
    gather_stage(0, 1)
    advance(1, 5)
    gather_stage(1, 0)
    for stage in range(2, 5):
        gather_stage(0, stage)
        gather_stage(1, stage - 1)
    gather_stage(1, 4)

    near_forward.wait_send()
    near_back.wait_send()
    for name, copies in swaps.items():
        if name not in ("mid", "gm"):
            for copy in copies:
                copy.wait_send()
    for b in range(2):
        for index in range(10):
            gather(b, index).wait_send()
        for slab in range(SLABS):
            for step in range(6):
                reduce_copy(b, slab, step, True).wait_send()
        for copy in stores(b):
            copy.wait()
    store_out.wait()
    store_grad.wait()


def whole_step(*operands):
    anywhere = pl.BlockSpec(memory_space=pl.ANY)
    bf16, f32 = jnp.bfloat16, jnp.float32
    frame_shape = jax.ShapeDtypeStruct((1, ROWS, WIDTH), bf16)
    totals_shape = (2, 2, 2, 2, 2, UNIT, HALF)
    conv_shape = jax.ShapeDtypeStruct((2, 2, 2, UNIT, 4 * WIDTH), bf16)
    proj_shape = jax.ShapeDtypeStruct((2, 2, 2, UNIT, WIDTH), bf16)
    frame = pltpu.VMEM((ROWS, WIDTH), bf16)
    double = pltpu.VMEM((ROWS, 2 * WIDTH), bf16)
    narrow = pltpu.VMEM((ROWS, WIDTH // 2), bf16)
    weight = pltpu.VMEM((WIDTH, 4 * WIDTH), bf16)
    square = pltpu.VMEM((WIDTH, WIDTH), bf16)
    padded = pltpu.VMEM((ROWS + NEAR, WIDTH), bf16)
    share = pltpu.VMEM((SLABS, WIDTH, TILE), bf16)
    dma = pltpu.SemaphoreType.DMA
    return pl.pallas_call(
        step_kernel,
        out_shape=[frame_shape, frame_shape] + [conv_shape, proj_shape] * 2,
        in_specs=[anywhere] * 6,
        out_specs=[anywhere] * 6,
        scratch_shapes=[
            weight, weight, square, square,
            padded, frame, frame, frame, frame, frame, frame,
            double, double, frame, frame,
            frame, frame, pltpu.VMEM((NEAR, WIDTH), bf16),
            pltpu.VMEM((ROWS, 2 * WIDTH), f32), pltpu.VMEM((ROWS, WIDTH), f32),
            padded, frame, frame, frame, frame, frame, narrow, frame, narrow,
            share, share, share, pltpu.VMEM(totals_shape, bf16),
            dma((21,)), dma((2,)), dma((2,)), dma((2, CHUNKS)), dma((2, CHUNKS)),
            dma((10, CHUNKS)), dma((10, CHUNKS)),
            dma((2, SLABS, 6)), dma((2, SLABS, 6)), dma((2, 10)), dma((2, 10)), dma((14,)),
        ],
        compiler_params=pltpu.CompilerParams(
            collective_id=0, has_side_effects=True, vmem_limit_bytes=67043328
        ),
    )(*operands)


def scaled(total):
    count = lax.axis_size("dp") * lax.axis_size(("tx", "ty")) * ROWS
    value = total.astype(jnp.float32) * float(count) ** (-0.5)
    return value.reshape(128, total.shape[-1])


def shards(*operands):
    block_output, input_gradient, *totals = whole_step(*operands)
    conv_two, proj_two, conv_one, proj_one = (scaled(total) for total in totals)
    return (block_output, input_gradient, conv_one, proj_one, conv_two, proj_two)


def solution(mesh):
    return jax.shard_map(
        shards,
        mesh=mesh,
        in_specs=(P("dp", ("tx", "ty"), None), P(), P(), P(), P(), P("dp", ("tx", "ty"), None)),
        out_specs=(
            P("dp", ("tx", "ty"), None),
            P("dp", ("tx", "ty"), None),
            P("ty", None),
            P("ty", None),
            P("ty", None),
            P("ty", None),
        ),
        check_vma=False,
    )
```

```python
import jax
import jax.numpy as jnp
from jax import lax
from jax.experimental import pallas as pl
from jax.experimental.pallas import tpu as pltpu
from jax.sharding import PartitionSpec as P

NEAR = 64
ROWS = 384
WIDTH = 1024
CHUNKS = 4
CHUNK = ROWS // CHUNKS
TILE = 256
HALVES = 2
HALF_ROWS = ROWS // HALVES

MESH = pl.DeviceIdType.MESH
UNIT = 16
HALF = 2560
SLABS = 10
ORDERS = (
    (
        (0, 2, 1, 4, 3, 5),
        (1, 5, 2, 3, 0, 4),
        (2, 0, 3, 5, 4, 1),
        (3, 1, 0, 2, 4, 5),
        (4, 5, 3, 1, 2, 0),
        (5, 3, 0, 2, 1, 4),
        (0, 3, 4, 5, 1, 2),
        (1, 5, 4, 2, 3, 0),
        (2, 4, 1, 5, 0, 3),
        (4, 3, 5, 0, 2, 1),
    ),
    (
        (1, 3, 5, 2, 4, 0),
        (0, 5, 3, 4, 2, 1),
        (3, 0, 1, 4, 5, 2),
        (2, 4, 0, 3, 1, 5),
        (5, 2, 1, 3, 0, 4),
        (4, 2, 5, 1, 0, 3),
        (1, 4, 3, 2, 0, 5),
        (0, 1, 2, 4, 5, 3),
        (3, 2, 0, 4, 1, 5),
        (5, 4, 2, 0, 1, 3),
    ),
)


def place():
    dp, tx, ty = (lax.axis_index(name) for name in ("dp", "tx", "ty"))
    y_hi, core = lax.div(dp, 2), lax.rem(dp, 2)
    y_lo, z = lax.div(ty, 4), lax.rem(ty, 4)
    zh, xh = lax.div(z, 2), lax.div(tx, 2)
    bits = (
        zh,
        lax.rem(zh + z, 2),
        y_hi,
        lax.rem(y_hi + y_lo, 2),
        xh,
        lax.rem(xh + tx, 2),
    )
    peers = (
        {"ty": y_lo * 4 + 3 - z},
        {"ty": y_lo * 4 + z + 1 - 2 * lax.rem(z, 2)},
        {"dp": (1 - y_hi) * 2 + core, "ty": (1 - y_lo) * 4 + z},
        {"ty": (1 - y_lo) * 4 + z},
        {"tx": 3 - tx},
        {"tx": tx + 1 - 2 * lax.rem(tx, 2)},
    )
    other_core = {"dp": y_hi * 2 + 1 - core}
    far_y = {"dp": (1 - y_hi) * 2 + core}
    return bits, core, peers, other_core, far_y


def remote(source, target, send_sem, recv_sem, peer):
    return pltpu.make_async_remote_copy(
        src_ref=source,
        dst_ref=target,
        send_sem=send_sem,
        recv_sem=recv_sem,
        device_id=peer,
        device_id_type=MESH,
    )


def dot_nn(left, right):
    return jnp.dot(left, right, preferred_element_type=jnp.float32)


def dot_nt(left, right):
    return lax.dot_general(
        left, right, (((1,), (1,)), ((), ())), preferred_element_type=jnp.float32
    )


def dot_tn(left, right):
    return lax.dot_general(
        left, right, (((0,), (0,)), ((), ())), preferred_element_type=jnp.float32
    )


def step_kernel(
    frames, conv_1, proj_1, conv_2, proj_2, out_grad,
    out_frames, frame_grad, conv_total_2, proj_total_2, conv_total_1, proj_total_1,
    w1, w2, q1, q2, xs, mid, s2, t1, t2, g, gmid, gp1, gp2, slope_t, slope_g,
    tap_in, tap_out, near_tap, pre2, wide,
    xs_in, mid_in, s2_in, t1_in, t2_in, gp2_in, g_in, gp1_in, gm_in,
    acc2, got2, got1, full,
    ld_sem, near_send, near_recv, far_send, far_recv, ex_send, ex_recv,
    rs_send, rs_recv, ag_send, ag_recv, st_sem,
):
    bf16, f32 = jnp.bfloat16, jnp.float32
    bits, core, peers, other_core, far_y = place()
    tx, ty = lax.axis_index("tx"), lax.axis_index("ty")
    index = tx * 8 + ty
    after, before = lax.rem(index + 1, 32), lax.rem(index + 31, 32)
    next_peer = {"tx": lax.div(after, 8), "ty": lax.rem(after, 8)}
    prev_peer = {"tx": lax.div(before, 8), "ty": lax.rem(before, 8)}
    later_peer = {"tx": lax.rem(tx + 1, 4)}
    earlier_peer = {"tx": lax.rem(tx + 3, 4)}
    first_shard, last_shard = index == 0, index == 31

    def load(index, source, target):
        return pltpu.make_async_copy(source, target, ld_sem.at[index])

    def columns(start):
        return pl.ds(pl.multiple_of(start, TILE), TILE)

    def conv_loads(j):
        return [
            load(
                4 * j + part,
                conv_1.at[:, pl.ds(part * WIDTH + j * TILE, TILE)],
                w1.at[:, pl.ds(part * WIDTH + j * TILE, TILE)],
            )
            for part in range(4)
        ]

    loads = {"x": load(16, frames.at[0], xs.at[pl.ds(NEAR, ROWS), :])}
    loads["q1"] = load(17, proj_1, q1)
    loads["w2"] = load(18, conv_2, w2)
    loads["g"] = load(19, out_grad.at[0], g)
    loads["q2"] = load(20, proj_2, q2)
    loads["x"].start()
    for j in range(4):
        for copy in conv_loads(j):
            copy.start()
    loads["q1"].start()

    barrier = pltpu.get_barrier_semaphore()
    for peer in peers + (other_core, far_y, next_peer, prev_peer):
        pl.semaphore_signal(barrier, inc=1, device_id=peer, device_id_type=MESH)
    pl.semaphore_wait(barrier, 10)

    def half(ref, which, width):
        return ref.at[:, pl.ds(pl.multiple_of(which * width, width), width)]

    def half_rows(ref, which, width, rows):
        return ref.at[rows, pl.ds(pl.multiple_of(which * width, width), width)]

    def swap(item, part, source, target):
        return remote(
            source, target, ex_send.at[item, part], ex_recv.at[item, part], other_core
        )

    every = slice(None)
    top = pl.ds(0, NEAR)
    parts = [pl.ds(c * CHUNK, CHUNK) for c in range(CHUNKS)]
    halves = [pl.ds(c * HALF_ROWS, HALF_ROWS) for c in range(HALVES)]
    swaps = {
        "x": [swap(0, 0, frames.at[0], xs_in.at[pl.ds(NEAR, ROWS), :])],
        "halo": [swap(1, 0, xs.at[top, :], xs_in.at[top, :])],
        "g": [swap(2, 0, half(out_grad.at[0], 1 - core, 512), g_in)],
    }
    for item, (name, source, target) in enumerate(
        (("t1", t1, t1_in), ("mid", mid, mid_in), ("s2", s2, s2_in), ("t2", t2, t2_in)), 3
    ):
        swaps[name] = [
            swap(item, c, source.at[rows, :], target.at[rows, :])
            for c, rows in enumerate(parts)
        ]
    for item, (name, source, target, width, pieces) in enumerate(
        (
            ("gp2", gp2, gp2_in, 1024, parts),
            ("gp1", gp1, gp1_in, 1024, halves),
            ("gm", gmid, gm_in, 512, halves),
        ),
        7,
    ):
        swaps[name] = [
            swap(item, c, half_rows(source, 1 - core, width, rows), target.at[rows, :])
            for c, rows in enumerate(pieces)
        ]

    near_forward = remote(
        frames.at[0, pl.ds(ROWS - NEAR, NEAR), :], xs.at[top, :],
        near_send.at[0], near_recv.at[0], next_peer,
    )
    near_back = remote(
        tap_out.at[top, :], near_tap, near_send.at[1], near_recv.at[1], prev_peer
    )
    far_forward = [
        remote(
            mid.at[rows, :], s2.at[rows, :], far_send.at[0, c], far_recv.at[0, c], later_peer
        )
        for c, rows in enumerate(parts)
    ]
    far_back = [
        remote(
            tap_out.at[rows, :], tap_in.at[rows, :],
            far_send.at[1, c], far_recv.at[1, c], earlier_peer,
        )
        for c, rows in enumerate(parts)
    ]

    near_forward.start()
    swaps["x"][0].start()
    swaps["g"][0].start()
    loads["x"].wait()
    near_forward.wait_recv()

    @pl.when(first_shard)
    def _():
        xs[0:NEAR, :] = jnp.zeros((NEAR, WIDTH), bf16)

    swaps["halo"][0].start()

    def tiles(count, body):
        def step(j, carry):
            body(j)
            return carry

        lax.fori_loop(0, count, step, 0)

    def first_forward(c):
        low = c * CHUNK
        rows = slice(low, low + CHUNK)
        moved = slice(NEAR + low, NEAR + low + CHUNK)

        def gate_tile(j):
            old, now = xs[rows, :], xs[moved, :]
            start = j * TILE
            a = dot_nn(old, w1[:, columns(start)]) + dot_nn(
                now, w1[:, columns(2 * WIDTH + start)]
            )
            v = dot_nn(old, w1[:, columns(WIDTH + start)]) + dot_nn(
                now, w1[:, columns(3 * WIDTH + start)]
            )
            th, gt = jnp.tanh(a), jax.nn.sigmoid(v)
            t1[rows, columns(start)] = (th * gt).astype(bf16)
            slope_t[rows, columns(start)] = (gt * (1.0 - th * th)).astype(bf16)
            slope_g[rows, columns(start)] = (th * gt * (1.0 - gt)).astype(bf16)

        if c == 0:
            for j in range(4):
                for copy in conv_loads(j):
                    copy.wait()
                gate_tile(j)
                if j == 0:
                    for name in ("w2", "g", "q2"):
                        loads[name].start()
            loads["q1"].wait()
        else:
            tiles(4, gate_tile)
        swaps["t1"][c].start()

        def out_tile(j):
            value = dot_nn(t1[rows, :], q1[:, columns(j * TILE)])
            value = value + xs[moved, columns(j * TILE)].astype(f32)
            mid[rows, columns(j * TILE)] = value.astype(bf16)

        tiles(4, out_tile)
        far_forward[c].start()
        swaps["mid"][c].start()

    for c in range(CHUNKS):
        first_forward(c)

    loads["w2"].wait()

    def pre_tile(j):
        pre2[:, columns(j * TILE)] = dot_nn(mid[...], w2[:, columns(2 * WIDTH + j * TILE)])

    tiles(8, pre_tile)
    loads["g"].wait()
    loads["q2"].wait()

    def gated_grad_tile(j):
        wide[:, columns(j * TILE)] = dot_nt(g[...], q2[columns(j * TILE), :])

    tiles(4, gated_grad_tile)

    def second_block(c):
        low = c * CHUNK
        rows = slice(low, low + CHUNK)
        far_forward[c].wait_recv()

        @pl.when(tx == 0)
        def _():
            s2[rows, :] = jnp.zeros((CHUNK, WIDTH), bf16)

        swaps["s2"][c].start()

        def gate_tile(j):
            old = s2[rows, :]
            here, there = columns(j * TILE), columns(WIDTH + j * TILE)
            a = dot_nn(old, w2[:, here]) + pre2[rows, here]
            v = dot_nn(old, w2[:, there]) + pre2[rows, there]
            th, gt = jnp.tanh(a), jax.nn.sigmoid(v)
            t2[rows, here] = (th * gt).astype(bf16)
            grad = wide[rows, here] * gt
            gp2[rows, here] = (grad * (1.0 - th * th)).astype(bf16)
            gp2[rows, there] = (grad * th * (1.0 - gt)).astype(bf16)

        tiles(4, gate_tile)
        swaps["t2"][c].start()
        swaps["gp2"][c].start()

        def tap_tile(j):
            value = dot_nt(gp2[rows, :], w2[columns(j * TILE), 0 : 2 * WIDTH])
            tap_out[rows, columns(j * TILE)] = value.astype(bf16)

        tiles(4, tap_tile)
        far_back[c].start()

    for c in range(CHUNKS):
        second_block(c)

    def units(start, count):
        return pl.ds(pl.multiple_of(start * UNIT, UNIT), count * UNIT)

    def ours(b, slab, rows):
        if b == 0:
            return acc2.at[slab, rows, :]
        return w2.at[rows, slab * TILE : slab * TILE + TILE]

    def theirs(b, slab, rows):
        return (got2, got1)[b].at[slab, rows, :]

    def weight_products(b, part):
        if b == 0:
            lefts = ((s2, 0, s2_in), (mid, 0, mid_in), (t2, 0, t2_in))
            own_p, own_g = half(gp2, core, 1024), half(g, core, 512)
            pre_in, grad_in = gp2_in, g_in
        else:
            lefts = ((xs, 0, xs_in), (xs, NEAR, xs_in), (t1, 0, t1_in))
            own_p, own_g = half(gp1, core, 1024), half(gmid, core, 512)
            pre_in, grad_in = gp1_in, gm_in
        def product_tile(m):
            own, low, partner = lefts[part]
            span = slice(low, low + ROWS)
            left = jnp.concatenate(
                [own[span, columns(m * TILE)], partner[span, columns(m * TILE)]], 0
            )
            for piece in range(2 if part < 2 else 1):
                lo = piece * 512
                if part < 2:
                    right = jnp.concatenate(
                        [own_p[:, lo : lo + 512], pre_in[:, lo : lo + 512]], 0
                    )
                else:
                    right = jnp.concatenate([own_g[...], grad_in[...]], 0)
                product = dot_tn(left, right).astype(bf16)
                first = part * 1024 + lo
                for row in range(16):
                    block = 2 * m + row // 8
                    y_lo, z = lax.div(block, 4), lax.rem(block, 4)
                    zh = lax.div(z, 2)
                    side = (row // 4) % 2
                    unit = (
                        zh,
                        lax.rem(zh + z, 2),
                        side,
                        lax.rem(side + y_lo, 2),
                        (row // 2) % 2,
                        row % 2,
                    )
                    for local in range(2):
                        slab = first // TILE + local
                        spot = 0
                        for step, dim in enumerate(ORDERS[b][slab]):
                            spot = spot + unit[dim] * 2 ** (5 - step)
                        ours(b, slab, units(spot, 1))[...] = product[
                            row * 16 : row * 16 + 16, local * TILE : local * TILE + TILE
                        ]

        tiles(4, product_tile)

    def ranges(b, slab, step):
        base = 0
        for earlier, dim in enumerate(ORDERS[b][slab][:step]):
            base = base + bits[dim] * 2 ** (5 - earlier)
        count = 2 ** (5 - step)
        mine = bits[ORDERS[b][slab][step]]
        return base + mine * count, base + (1 - mine) * count, count

    def reduce_copy(b, slab, step, landing):
        keep, give, count = ranges(b, slab, step)
        return remote(
            ours(b, slab, units(give, count)),
            theirs(b, slab, units(keep if landing else give, count)),
            rs_send.at[b, slab, step], rs_recv.at[b, slab, step],
            peers[ORDERS[b][slab][step]],
        )

    yh, xh, xq = bits[2], bits[4], bits[5]

    def fold(b, slab, step):
        keep, give, count = ranges(b, slab, step)
        chunk = min(count, 16)

        def total(i):
            here = ours(b, slab, units(keep + i * chunk, chunk))[...]
            return here + theirs(b, slab, units(give + i * chunk, chunk))[...]

        if step == 5:
            full[b, core, yh, xh, xq, :, slab * TILE : slab * TILE + TILE] = total(0)
            return
        for i in range(count // chunk):
            ours(b, slab, units(keep + i * chunk, chunk))[...] = total(i)

    def slabs_of(part):
        return range(4 * part, min(4 * part + 4, SLABS))

    def advance(b, step, slabs=range(SLABS)):
        for slab in slabs:
            reduce_copy(b, slab, step, False).wait_recv()
            fold(b, slab, step)
            if step < 5:
                reduce_copy(b, slab, step + 1, True).start()

    def begin_reduce(b, part):
        for slab in slabs_of(part):
            reduce_copy(b, slab, 0, True).start()

    for name in ("mid", "s2", "t2", "gp2", "g"):
        for copy in swaps[name]:
            copy.wait_recv()
    for part in range(3):
        weight_products(0, part)
        begin_reduce(0, part)

    def current_tile(j):
        value = dot_nt(gp2[...], w2[columns(j * TILE), 2 * WIDTH : 4 * WIDTH])
        wide[:, columns(j * TILE)] = value + g[:, columns(j * TILE)].astype(f32)

    tiles(4, current_tile)

    def first_backward(c):
        low = c * HALF_ROWS
        rows = slice(low, low + HALF_ROWS)
        for copy in far_back[c * CHUNKS // HALVES : (c + 1) * CHUNKS // HALVES]:
            copy.wait_recv()
        tap = tap_in[rows, :].astype(f32)
        total = wide[rows, :] + jnp.where(tx == 3, 0.0, tap)
        gmid[rows, :] = total.astype(bf16)
        swaps["gm"][c].start()

        def slope_tile(j):
            here, there = columns(j * TILE), columns(WIDTH + j * TILE)
            grad = dot_nt(gmid[rows, :], q1[here, :])
            gp1[rows, here] = (grad * slope_t[rows, here].astype(f32)).astype(bf16)
            gp1[rows, there] = (grad * slope_g[rows, here].astype(f32)).astype(bf16)

        tiles(4, slope_tile)
        swaps["gp1"][c].start()

    for c in range(HALVES):
        first_backward(c)
    for copy in far_forward + swaps["mid"]:
        copy.wait_send()

    def second_out_tile(j):
        value = dot_nn(t2[...], q2[:, columns(j * TILE)])
        mid[:, columns(j * TILE)] = (value + mid[:, columns(j * TILE)].astype(f32)).astype(bf16)

    tiles(4, second_out_tile)
    store_out = pltpu.make_async_copy(mid, out_frames.at[0], st_sem.at[0])
    store_out.start()
    for name in ("x", "halo", "t1", "gp1", "gm"):
        for copy in swaps[name]:
            copy.wait_recv()
    for part in range(3):
        weight_products(1, part)
        begin_reduce(1, part)
        advance(0, 0, slabs_of(part))

    for copy in far_back:
        copy.wait_send()

    def first_tap_tile(j):
        value = dot_nt(gp1[...], w1[columns(j * TILE), 0 : 2 * WIDTH])
        tap_out[:, columns(j * TILE)] = value.astype(bf16)

    tiles(4, first_tap_tile)
    near_back.start()

    def first_current_tile(j):
        value = dot_nt(gp1[...], w1[columns(j * TILE), 2 * WIDTH : 4 * WIDTH])
        pre2[:, columns(j * TILE)] = value + gmid[:, columns(j * TILE)].astype(f32)

    tiles(4, first_current_tile)
    advance(0, 1)
    advance(1, 0)
    advance(0, 2)
    near_back.wait_recv()
    for copy in swaps["gm"]:
        copy.wait_send()
    body_rows = ROWS - NEAR
    gmid[0:body_rows, :] = (
        pre2[0:body_rows, 0:WIDTH] + tap_out[NEAR:ROWS, :].astype(f32)
    ).astype(bf16)
    edge = jnp.where(last_shard, 0.0, near_tap[...].astype(f32))
    gmid[body_rows:ROWS, :] = (pre2[body_rows:ROWS, 0:WIDTH] + edge).astype(bf16)
    store_grad = pltpu.make_async_copy(gmid, frame_grad.at[0], st_sem.at[1])
    store_grad.start()

    left, right = slice(0, HALF // 2), slice(HALF // 2, HALF)

    def gather_copy(b, index, where, target):
        ref = full.at[(b, core) + where]
        return remote(ref, ref, ag_send.at[b, index], ag_recv.at[b, index], target)

    places = (
        ((yh, xh, xq), far_y),
        ((every, xh, xq, every, left), peers[5]),
        ((every, xh, xq, every, right), peers[4]),
        ((every, xh, every, every, left), peers[4]),
        ((every, every, xq, every, right), peers[5]),
        ((every, xh, xq), other_core),
        ((every, xh, 1 - xq, every, left), other_core),
        ((every, 1 - xh, xq, every, right), other_core),
        ((every, 1 - xh, every, every, left), other_core),
        ((every, every, 1 - xq, every, right), other_core),
    )

    def gather(b, index):
        return gather_copy(b, index, *places[index])

    def stores(b):
        conv, proj = ((conv_total_2, proj_total_2), (conv_total_1, proj_total_1))[b]
        copies = []
        for k in range(2):
            moves = (
                (conv, k * 1024, 0, 1024),
                (conv, 2048 + k * 1024, 1024, 1024),
                (proj, k * 512, 2048, 512),
            )
            for target, to, start, width in moves:
                copies.append(
                    pltpu.make_async_copy(
                        full.at[b, k, :, :, :, :, start : start + width],
                        target.at[:, :, :, :, to : to + width],
                        st_sem.at[2 + b * 6 + len(copies)],
                    )
                )
        return copies

    def gather_stage(b, stage):
        waits = ((), (0,), (1, 2), (3, 4), (5, 6, 7, 8, 9))[stage]
        starts = ((0,), (1, 2, 5), (3, 4, 6, 7), (8, 9), ())[stage]
        for index in waits:
            gather(b, index).wait_recv()
        for index in starts:
            gather(b, index).start()
        if stage == 4:
            for copy in stores(b):
                copy.start()

    advance(1, 1)
    advance(0, 3)
    advance(1, 2)
    advance(0, 4)
    advance(1, 3)
    advance(0, 5)
    gather_stage(0, 0)
    advance(1, 4)
    gather_stage(0, 1)
    advance(1, 5)
    gather_stage(1, 0)
    for stage in range(2, 5):
        gather_stage(0, stage)
        gather_stage(1, stage - 1)
    gather_stage(1, 4)

    near_forward.wait_send()
    near_back.wait_send()
    for name, copies in swaps.items():
        if name not in ("mid", "gm"):
            for copy in copies:
                copy.wait_send()
    for b in range(2):
        for index in range(10):
            gather(b, index).wait_send()
        for slab in range(SLABS):
            for step in range(6):
                reduce_copy(b, slab, step, True).wait_send()
        for copy in stores(b):
            copy.wait()
    store_out.wait()
    store_grad.wait()


def whole_step(*operands):
    anywhere = pl.BlockSpec(memory_space=pl.ANY)
    bf16, f32 = jnp.bfloat16, jnp.float32
    frame_shape = jax.ShapeDtypeStruct((1, ROWS, WIDTH), bf16)
    totals_shape = (2, 2, 2, 2, 2, UNIT, HALF)
    conv_shape = jax.ShapeDtypeStruct((2, 2, 2, UNIT, 4 * WIDTH), bf16)
    proj_shape = jax.ShapeDtypeStruct((2, 2, 2, UNIT, WIDTH), bf16)
    frame = pltpu.VMEM((ROWS, WIDTH), bf16)
    double = pltpu.VMEM((ROWS, 2 * WIDTH), bf16)
    narrow = pltpu.VMEM((ROWS, WIDTH // 2), bf16)
    weight = pltpu.VMEM((WIDTH, 4 * WIDTH), bf16)
    square = pltpu.VMEM((WIDTH, WIDTH), bf16)
    padded = pltpu.VMEM((ROWS + NEAR, WIDTH), bf16)
    share = pltpu.VMEM((SLABS, WIDTH, TILE), bf16)
    dma = pltpu.SemaphoreType.DMA
    return pl.pallas_call(
        step_kernel,
        out_shape=[frame_shape, frame_shape] + [conv_shape, proj_shape] * 2,
        in_specs=[anywhere] * 6,
        out_specs=[anywhere] * 6,
        scratch_shapes=[
            weight, weight, square, square,
            padded, frame, frame, frame, frame, frame, frame,
            double, double, frame, frame,
            frame, frame, pltpu.VMEM((NEAR, WIDTH), bf16),
            pltpu.VMEM((ROWS, 2 * WIDTH), f32), pltpu.VMEM((ROWS, WIDTH), f32),
            padded, frame, frame, frame, frame, frame, narrow, frame, narrow,
            share, share, share, pltpu.VMEM(totals_shape, bf16),
            dma((21,)), dma((2,)), dma((2,)), dma((2, CHUNKS)), dma((2, CHUNKS)),
            dma((10, CHUNKS)), dma((10, CHUNKS)),
            dma((2, SLABS, 6)), dma((2, SLABS, 6)), dma((2, 10)), dma((2, 10)), dma((14,)),
        ],
        compiler_params=pltpu.CompilerParams(
            collective_id=0, has_side_effects=True, vmem_limit_bytes=67043328
        ),
    )(*operands)


def scaled(total):
    count = lax.axis_size("dp") * lax.axis_size(("tx", "ty")) * ROWS
    value = total.astype(jnp.float32) * float(count) ** (-0.5)
    return value.reshape(128, total.shape[-1])


def shards(*operands):
    block_output, input_gradient, *totals = whole_step(*operands)
    conv_two, proj_two, conv_one, proj_one = (scaled(total) for total in totals)
    return (block_output, input_gradient, conv_one, proj_one, conv_two, proj_two)


def solution(mesh):
    return jax.shard_map(
        shards,
        mesh=mesh,
        in_specs=(P("dp", ("tx", "ty"), None), P(), P(), P(), P(), P("dp", ("tx", "ty"), None)),
        out_specs=(
            P("dp", ("tx", "ty"), None),
            P("dp", ("tx", "ty"), None),
            P("ty", None),
            P("ty", None),
            P("ty", None),
            P("ty", None),
        ),
        check_vma=False,
    )
```

```python
import jax
import jax.numpy as jnp
from jax import lax
from jax.experimental import pallas as pl
from jax.experimental.pallas import tpu as pltpu
from jax.sharding import PartitionSpec as P

NEAR = 64
ROWS = 384
WIDTH = 1024
CHUNKS = 3
CHUNK = ROWS // CHUNKS
TILE = 256
BROAD = 512
HALVES = 2
HALF_ROWS = ROWS // HALVES

MESH = pl.DeviceIdType.MESH
UNIT = 16
HALF = 2560
SLABS = 10
ORDERS = (
    (
        (0, 2, 1, 4, 3, 5),
        (1, 5, 2, 3, 0, 4),
        (2, 0, 3, 5, 4, 1),
        (3, 1, 0, 2, 4, 5),
        (4, 5, 3, 1, 2, 0),
        (5, 3, 0, 2, 1, 4),
        (0, 3, 4, 5, 1, 2),
        (1, 5, 4, 2, 3, 0),
        (2, 4, 1, 5, 0, 3),
        (4, 3, 5, 0, 2, 1),
    ),
    (
        (1, 3, 5, 2, 4, 0),
        (0, 5, 3, 4, 2, 1),
        (3, 0, 1, 4, 5, 2),
        (2, 4, 0, 3, 1, 5),
        (5, 2, 1, 3, 0, 4),
        (4, 2, 5, 1, 0, 3),
        (1, 4, 3, 2, 0, 5),
        (0, 1, 2, 4, 5, 3),
        (3, 2, 0, 4, 1, 5),
        (5, 4, 2, 0, 1, 3),
    ),
)


def place():
    dp, tx, ty = (lax.axis_index(name) for name in ("dp", "tx", "ty"))
    y_hi, core = lax.div(dp, 2), lax.rem(dp, 2)
    y_lo, z = lax.div(ty, 4), lax.rem(ty, 4)
    zh, xh = lax.div(z, 2), lax.div(tx, 2)
    bits = (
        zh,
        lax.rem(zh + z, 2),
        y_hi,
        lax.rem(y_hi + y_lo, 2),
        xh,
        lax.rem(xh + tx, 2),
    )
    peers = (
        {"ty": y_lo * 4 + 3 - z},
        {"ty": y_lo * 4 + z + 1 - 2 * lax.rem(z, 2)},
        {"dp": (1 - y_hi) * 2 + core, "ty": (1 - y_lo) * 4 + z},
        {"ty": (1 - y_lo) * 4 + z},
        {"tx": 3 - tx},
        {"tx": tx + 1 - 2 * lax.rem(tx, 2)},
    )
    other_core = {"dp": y_hi * 2 + 1 - core}
    far_y = {"dp": (1 - y_hi) * 2 + core}
    return bits, core, peers, other_core, far_y


def remote(source, target, send_sem, recv_sem, peer):
    return pltpu.make_async_remote_copy(
        src_ref=source,
        dst_ref=target,
        send_sem=send_sem,
        recv_sem=recv_sem,
        device_id=peer,
        device_id_type=MESH,
    )


def dot_nn(left, right):
    return jnp.dot(left, right, preferred_element_type=jnp.float32)


def dot_nt(left, right):
    return lax.dot_general(
        left, right, (((1,), (1,)), ((), ())), preferred_element_type=jnp.float32
    )


def dot_tn(left, right):
    return lax.dot_general(
        left, right, (((0,), (0,)), ((), ())), preferred_element_type=jnp.float32
    )


def step_kernel(
    frames, conv_1, proj_1, conv_2, proj_2, out_grad,
    out_frames, frame_grad, conv_total_2, proj_total_2, conv_total_1, proj_total_1,
    w1, w2, q1, q2, xs, mid, s2, t1, t2, g, gmid, gp1, gp2, slope_t, slope_g,
    tap_in, tap_out, near_tap, pre2, wide,
    xs_in, mid_in, s2_in, t1_in, t2_in, gp2_in, g_in, gp1_in, gm_in,
    acc2, got2, got1, full,
    ld_sem, near_send, near_recv, far_send, far_recv, ex_send, ex_recv,
    rs_send, rs_recv, ag_send, ag_recv, st_sem,
):
    bf16, f32 = jnp.bfloat16, jnp.float32
    bits, core, peers, other_core, far_y = place()
    tx, ty = lax.axis_index("tx"), lax.axis_index("ty")
    index = tx * 8 + ty
    after, before = lax.rem(index + 1, 32), lax.rem(index + 31, 32)
    next_peer = {"tx": lax.div(after, 8), "ty": lax.rem(after, 8)}
    prev_peer = {"tx": lax.div(before, 8), "ty": lax.rem(before, 8)}
    later_peer = {"tx": lax.rem(tx + 1, 4)}
    earlier_peer = {"tx": lax.rem(tx + 3, 4)}
    first_shard, last_shard = index == 0, index == 31

    def load(index, source, target):
        return pltpu.make_async_copy(source, target, ld_sem.at[index])

    def columns(start):
        return pl.ds(pl.multiple_of(start, TILE), TILE)

    def broad(start):
        return pl.ds(pl.multiple_of(start, BROAD), BROAD)

    def conv_loads(j):
        return [
            load(
                4 * j + part,
                conv_1.at[:, pl.ds(part * WIDTH + j * TILE, TILE)],
                w1.at[:, pl.ds(part * WIDTH + j * TILE, TILE)],
            )
            for part in range(4)
        ]

    loads = {"x": load(16, frames.at[0], xs.at[pl.ds(NEAR, ROWS), :])}
    loads["q1"] = load(17, proj_1, q1)
    loads["w2"] = load(18, conv_2, w2)
    loads["g"] = load(19, out_grad.at[0], g)
    loads["q2"] = load(20, proj_2, q2)
    barrier = pltpu.get_barrier_semaphore()
    for peer in peers + (other_core, far_y, next_peer, prev_peer):
        pl.semaphore_signal(barrier, inc=1, device_id=peer, device_id_type=MESH)
    loads["x"].start()
    pl.semaphore_wait(barrier, 10)
    near_forward = remote(
        frames.at[0, pl.ds(ROWS - NEAR, NEAR), :], xs.at[pl.ds(0, NEAR), :],
        near_send.at[0], near_recv.at[0], next_peer,
    )
    near_forward.start()
    for j in range(4):
        for copy in conv_loads(j):
            copy.start()
    loads["q1"].start()

    def half(ref, which, width):
        return ref.at[:, pl.ds(pl.multiple_of(which * width, width), width)]

    def half_rows(ref, which, width, rows):
        return ref.at[rows, pl.ds(pl.multiple_of(which * width, width), width)]

    def swap(item, part, source, target):
        return remote(
            source, target, ex_send.at[item, part], ex_recv.at[item, part], other_core
        )

    every = slice(None)
    top = pl.ds(0, NEAR)
    parts = [pl.ds(c * CHUNK, CHUNK) for c in range(CHUNKS)]
    halves = [pl.ds(c * HALF_ROWS, HALF_ROWS) for c in range(HALVES)]
    swaps = {
        "x": [swap(0, 0, frames.at[0], xs_in.at[pl.ds(NEAR, ROWS), :])],
        "halo": [swap(1, 0, xs.at[top, :], xs_in.at[top, :])],
        "g": [swap(2, 0, half(out_grad.at[0], 1 - core, 512), g_in)],
    }
    for item, (name, source, target) in enumerate(
        (("t1", t1, t1_in), ("mid", mid, mid_in), ("s2", s2, s2_in), ("t2", t2, t2_in)), 3
    ):
        swaps[name] = [
            swap(item, c, source.at[rows, :], target.at[rows, :])
            for c, rows in enumerate(parts)
        ]
    for item, (name, source, target, width, pieces) in enumerate(
        (
            ("gp2", gp2, gp2_in, 1024, parts),
            ("gp1", gp1, gp1_in, 1024, halves),
            ("gm", gmid, gm_in, 512, halves),
        ),
        7,
    ):
        swaps[name] = [
            swap(item, c, half_rows(source, 1 - core, width, rows), target.at[rows, :])
            for c, rows in enumerate(pieces)
        ]

    near_back = remote(
        tap_out.at[top, :], near_tap, near_send.at[1], near_recv.at[1], prev_peer
    )
    far_forward = [
        remote(
            mid.at[rows, :], s2.at[rows, :], far_send.at[0, c], far_recv.at[0, c], later_peer
        )
        for c, rows in enumerate(parts)
    ]
    far_back = [
        remote(
            tap_out.at[rows, :], tap_in.at[rows, :],
            far_send.at[1, c], far_recv.at[1, c], earlier_peer,
        )
        for c, rows in enumerate(parts)
    ]

    loads["x"].wait()

    def share_inputs():
        swaps["x"][0].start()
        swaps["g"][0].start()

    def take_halo():
        near_forward.wait_recv()

        @pl.when(first_shard)
        def _():
            xs[0:NEAR, :] = jnp.zeros((NEAR, WIDTH), bf16)

        swaps["halo"][0].start()

    def tiles(count, body):
        def step(j, carry):
            body(j)
            return carry

        lax.fori_loop(0, count, step, 0)

    def first_forward(c):
        low = c * CHUNK
        rows = slice(low, low + CHUNK)
        moved = slice(NEAR + low, NEAR + low + CHUNK)

        def gate_tile(j):
            old, now = xs[rows, :], xs[moved, :]
            start = j * TILE
            a = dot_nn(old, w1[:, columns(start)]) + dot_nn(
                now, w1[:, columns(2 * WIDTH + start)]
            )
            v = dot_nn(old, w1[:, columns(WIDTH + start)]) + dot_nn(
                now, w1[:, columns(3 * WIDTH + start)]
            )
            th, gt = jnp.tanh(a), jax.nn.sigmoid(v)
            t1[rows, columns(start)] = (th * gt).astype(bf16)
            slope_t[rows, columns(start)] = (gt * (1.0 - th * th)).astype(bf16)
            slope_g[rows, columns(start)] = (th * gt * (1.0 - gt)).astype(bf16)

        if c == 1:
            for j in range(4):
                for copy in conv_loads(j):
                    copy.wait()
                gate_tile(j)
                if j == 0:
                    for name in ("w2", "g", "q2"):
                        loads[name].start()
            loads["q1"].wait()
            share_inputs()
        else:
            if c == 0:
                take_halo()
            tiles(4, gate_tile)
        swaps["t1"][c].start()

        def out_tile(j):
            value = dot_nn(t1[rows, :], q1[:, columns(j * TILE)])
            value = value + xs[moved, columns(j * TILE)].astype(f32)
            mid[rows, columns(j * TILE)] = value.astype(bf16)

        tiles(4, out_tile)
        far_forward[c].start()
        swaps["mid"][c].start()

    turns = (1, 2, 0)
    for c in turns:
        first_forward(c)

    loads["w2"].wait()

    def pre_tile(j):
        pre2[:, broad(j * BROAD)] = dot_nn(mid[...], w2[:, broad(2 * WIDTH + j * BROAD)])

    tiles(4, pre_tile)
    loads["g"].wait()
    loads["q2"].wait()

    def gated_grad_tile(j):
        wide[:, broad(j * BROAD)] = dot_nt(g[...], q2[broad(j * BROAD), :])

    tiles(2, gated_grad_tile)

    def second_block(c):
        low = c * CHUNK
        rows = slice(low, low + CHUNK)
        far_forward[c].wait_recv()

        @pl.when(tx == 0)
        def _():
            s2[rows, :] = jnp.zeros((CHUNK, WIDTH), bf16)

        swaps["s2"][c].start()

        def gate_tile(j):
            old = s2[rows, :]
            here, there = columns(j * TILE), columns(WIDTH + j * TILE)
            a = dot_nn(old, w2[:, here]) + pre2[rows, here]
            v = dot_nn(old, w2[:, there]) + pre2[rows, there]
            th, gt = jnp.tanh(a), jax.nn.sigmoid(v)
            t2[rows, here] = (th * gt).astype(bf16)
            grad = wide[rows, here] * gt
            gp2[rows, here] = (grad * (1.0 - th * th)).astype(bf16)
            gp2[rows, there] = (grad * th * (1.0 - gt)).astype(bf16)

        tiles(4, gate_tile)
        swaps["t2"][c].start()
        swaps["gp2"][c].start()

        def tap_tile(j):
            value = dot_nt(gp2[rows, :], w2[columns(j * TILE), 0 : 2 * WIDTH])
            tap_out[rows, columns(j * TILE)] = value.astype(bf16)

        tiles(4, tap_tile)
        far_back[c].start()

    for c in turns:
        second_block(c)

    def units(start, count):
        return pl.ds(pl.multiple_of(start * UNIT, UNIT), count * UNIT)

    def ours(b, slab, rows):
        if b == 0:
            return acc2.at[slab, rows, :]
        return w2.at[rows, slab * TILE : slab * TILE + TILE]

    def theirs(b, slab, rows):
        return (got2, got1)[b].at[slab, rows, :]

    def weight_products(b, part):
        if b == 0:
            lefts = ((s2, 0, s2_in), (mid, 0, mid_in), (t2, 0, t2_in))
            own_p, own_g = half(gp2, core, 1024), half(g, core, 512)
            pre_in, grad_in = gp2_in, g_in
        else:
            lefts = ((xs, 0, xs_in), (xs, NEAR, xs_in), (t1, 0, t1_in))
            own_p, own_g = half(gp1, core, 1024), half(gmid, core, 512)
            pre_in, grad_in = gp1_in, gm_in
        def product_tile(m):
            own, low, partner = lefts[part]
            span = slice(low, low + ROWS)
            left = jnp.concatenate(
                [own[span, columns(m * TILE)], partner[span, columns(m * TILE)]], 0
            )
            for piece in range(2 if part < 2 else 1):
                lo = piece * 512
                if part < 2:
                    right = jnp.concatenate(
                        [own_p[:, lo : lo + 512], pre_in[:, lo : lo + 512]], 0
                    )
                else:
                    right = jnp.concatenate([own_g[...], grad_in[...]], 0)
                product = dot_tn(left, right).astype(bf16)
                first = part * 1024 + lo
                for row in range(16):
                    block = 2 * m + row // 8
                    y_lo, z = lax.div(block, 4), lax.rem(block, 4)
                    zh = lax.div(z, 2)
                    side = (row // 4) % 2
                    unit = (
                        zh,
                        lax.rem(zh + z, 2),
                        side,
                        lax.rem(side + y_lo, 2),
                        (row // 2) % 2,
                        row % 2,
                    )
                    for local in range(2):
                        slab = first // TILE + local
                        spot = 0
                        for step, dim in enumerate(ORDERS[b][slab]):
                            spot = spot + unit[dim] * 2 ** (5 - step)
                        ours(b, slab, units(spot, 1))[...] = product[
                            row * 16 : row * 16 + 16, local * TILE : local * TILE + TILE
                        ]

        tiles(4, product_tile)

    def ranges(b, slab, step):
        base = 0
        for earlier, dim in enumerate(ORDERS[b][slab][:step]):
            base = base + bits[dim] * 2 ** (5 - earlier)
        count = 2 ** (5 - step)
        mine = bits[ORDERS[b][slab][step]]
        return base + mine * count, base + (1 - mine) * count, count

    def reduce_copy(b, slab, step, landing):
        keep, give, count = ranges(b, slab, step)
        return remote(
            ours(b, slab, units(give, count)),
            theirs(b, slab, units(keep if landing else give, count)),
            rs_send.at[b, slab, step % 2], rs_recv.at[b, slab, step],
            peers[ORDERS[b][slab][step]],
        )

    yh, xh, xq = bits[2], bits[4], bits[5]

    def fold(b, slab, step):
        keep, give, count = ranges(b, slab, step)
        chunk = min(count, 16)

        def total(i):
            here = ours(b, slab, units(keep + i * chunk, chunk))[...]
            return here + theirs(b, slab, units(give + i * chunk, chunk))[...]

        if step == 5:
            full[b, core, yh, xh, xq, :, slab * TILE : slab * TILE + TILE] = total(0)
            return
        for i in range(count // chunk):
            ours(b, slab, units(keep + i * chunk, chunk))[...] = total(i)

    def slabs_of(part):
        return range(4 * part, min(4 * part + 4, SLABS))

    def advance(b, step, slabs=range(SLABS)):
        for slab in slabs:
            reduce_copy(b, slab, step, False).wait_recv()
            fold(b, slab, step)
            if step < 5:
                reduce_copy(b, slab, step + 1, True).start()
        for slab in slabs:
            reduce_copy(b, slab, step, True).wait_send()

    def begin_reduce(b, part):
        for slab in slabs_of(part):
            reduce_copy(b, slab, 0, True).start()

    for name in ("mid", "s2", "t2", "gp2", "g"):
        for copy in swaps[name]:
            copy.wait_recv()
    for part in range(3):
        weight_products(0, part)
        begin_reduce(0, part)

    def current_tile(j):
        value = dot_nt(gp2[...], w2[broad(j * BROAD), 2 * WIDTH : 4 * WIDTH])
        wide[:, broad(j * BROAD)] = value + g[:, broad(j * BROAD)].astype(f32)

    tiles(2, current_tile)

    def first_backward(c):
        low = c * HALF_ROWS
        rows = slice(low, low + HALF_ROWS)
        tap = tap_in[rows, :].astype(f32)
        total = wide[rows, :] + jnp.where(tx == 3, 0.0, tap)
        gmid[rows, :] = total.astype(bf16)
        swaps["gm"][c].start()

        def slope_tile(j):
            here, there = columns(j * TILE), columns(WIDTH + j * TILE)
            grad = dot_nt(gmid[rows, :], q1[here, :])
            gp1[rows, here] = (grad * slope_t[rows, here].astype(f32)).astype(bf16)
            gp1[rows, there] = (grad * slope_g[rows, here].astype(f32)).astype(bf16)

        tiles(4, slope_tile)
        swaps["gp1"][c].start()

    for copy in far_back:
        copy.wait_recv()
    for c in range(HALVES):
        first_backward(c)
    for copy in far_forward + swaps["mid"]:
        copy.wait_send()

    def second_out_tile(j):
        value = dot_nn(t2[...], q2[:, broad(j * BROAD)])
        mid[:, broad(j * BROAD)] = (value + mid[:, broad(j * BROAD)].astype(f32)).astype(bf16)

    tiles(2, second_out_tile)
    store_out = pltpu.make_async_copy(mid, out_frames.at[0], st_sem.at[0])
    store_out.start()
    advance(0, 0)
    for name in ("x", "halo", "t1", "gp1", "gm"):
        for copy in swaps[name]:
            copy.wait_recv()
    for part in range(3):
        weight_products(1, part)
        begin_reduce(1, part)
    advance(0, 1)

    for copy in far_back:
        copy.wait_send()

    def first_tap_tile(j):
        value = dot_nt(gp1[...], w1[broad(j * BROAD), 0 : 2 * WIDTH])
        tap_out[:, broad(j * BROAD)] = value.astype(bf16)

    tiles(2, first_tap_tile)
    near_back.start()

    def first_current_tile(j):
        value = dot_nt(gp1[...], w1[broad(j * BROAD), 2 * WIDTH : 4 * WIDTH])
        pre2[:, broad(j * BROAD)] = value + gmid[:, broad(j * BROAD)].astype(f32)

    tiles(2, first_current_tile)
    advance(1, 0)
    advance(0, 2)
    near_back.wait_recv()
    for copy in swaps["gm"]:
        copy.wait_send()
    body_rows = ROWS - NEAR
    gmid[0:body_rows, :] = (
        pre2[0:body_rows, 0:WIDTH] + tap_out[NEAR:ROWS, :].astype(f32)
    ).astype(bf16)
    edge = jnp.where(last_shard, 0.0, near_tap[...].astype(f32))
    gmid[body_rows:ROWS, :] = (pre2[body_rows:ROWS, 0:WIDTH] + edge).astype(bf16)
    store_grad = pltpu.make_async_copy(gmid, frame_grad.at[0], st_sem.at[1])
    store_grad.start()

    left, right = slice(0, HALF // 2), slice(HALF // 2, HALF)

    def gather_copy(b, index, where, target):
        ref = full.at[(b, core) + where]
        return remote(ref, ref, ag_send.at[b, index], ag_recv.at[b, index], target)

    places = (
        ((yh, xh, xq), far_y),
        ((every, xh, xq, every, left), peers[5]),
        ((every, xh, xq, every, right), peers[4]),
        ((every, xh, every, every, left), peers[4]),
        ((every, every, xq, every, right), peers[5]),
        ((every, xh, xq), other_core),
        ((every, xh, 1 - xq, every, left), other_core),
        ((every, 1 - xh, xq, every, right), other_core),
        ((every, 1 - xh, every, every, left), other_core),
        ((every, every, 1 - xq, every, right), other_core),
    )

    def gather(b, index):
        return gather_copy(b, index, *places[index])

    def stores(b):
        conv, proj = ((conv_total_2, proj_total_2), (conv_total_1, proj_total_1))[b]
        copies = []
        for k in range(2):
            moves = (
                (conv, k * 1024, 0, 1024),
                (conv, 2048 + k * 1024, 1024, 1024),
                (proj, k * 512, 2048, 512),
            )
            for target, to, start, width in moves:
                copies.append(
                    pltpu.make_async_copy(
                        full.at[b, k, :, :, :, :, start : start + width],
                        target.at[:, :, :, :, to : to + width],
                        st_sem.at[2 + b * 6 + len(copies)],
                    )
                )
        return copies

    def gather_stage(b, stage):
        waits = ((), (0,), (1, 2), (3, 4), (5, 6, 7, 8, 9))[stage]
        starts = ((0,), (1, 2, 5), (3, 4, 6, 7), (8, 9), ())[stage]
        for index in waits:
            gather(b, index).wait_recv()
        for index in starts:
            gather(b, index).start()
        if stage == 4:
            for copy in stores(b):
                copy.start()

    for step in range(1, 4):
        advance(1, step)
        advance(0, step + 2)
    gather_stage(0, 0)
    advance(1, 4)
    advance(1, 5)
    gather_stage(1, 0)
    gather_stage(0, 1)
    gather_stage(1, 1)
    gather_stage(0, 2)
    gather_stage(1, 2)
    gather_stage(0, 3)
    near_forward.wait_send()
    near_back.wait_send()
    for name, copies in swaps.items():
        if name not in ("mid", "gm"):
            for copy in copies:
                copy.wait_send()
    store_out.wait()
    store_grad.wait()
    gather_stage(0, 4)
    gather_stage(1, 3)
    gather_stage(1, 4)

    for b in range(2):
        for index in range(10):
            gather(b, index).wait_send()
        for copy in stores(b):
            copy.wait()


def whole_step(*operands):
    anywhere = pl.BlockSpec(memory_space=pl.ANY)
    bf16, f32 = jnp.bfloat16, jnp.float32
    frame_shape = jax.ShapeDtypeStruct((1, ROWS, WIDTH), bf16)
    totals_shape = (2, 2, 2, 2, 2, UNIT, HALF)
    conv_shape = jax.ShapeDtypeStruct((2, 2, 2, UNIT, 4 * WIDTH), bf16)
    proj_shape = jax.ShapeDtypeStruct((2, 2, 2, UNIT, WIDTH), bf16)
    frame = pltpu.VMEM((ROWS, WIDTH), bf16)
    double = pltpu.VMEM((ROWS, 2 * WIDTH), bf16)
    narrow = pltpu.VMEM((ROWS, WIDTH // 2), bf16)
    weight = pltpu.VMEM((WIDTH, 4 * WIDTH), bf16)
    square = pltpu.VMEM((WIDTH, WIDTH), bf16)
    padded = pltpu.VMEM((ROWS + NEAR, WIDTH), bf16)
    share = pltpu.VMEM((SLABS, WIDTH, TILE), bf16)
    dma = pltpu.SemaphoreType.DMA
    return pl.pallas_call(
        step_kernel,
        out_shape=[frame_shape, frame_shape] + [conv_shape, proj_shape] * 2,
        in_specs=[anywhere] * 6,
        out_specs=[anywhere] * 6,
        scratch_shapes=[
            weight, weight, square, square,
            padded, frame, frame, frame, frame, frame, frame,
            double, double, frame, frame,
            frame, frame, pltpu.VMEM((NEAR, WIDTH), bf16),
            pltpu.VMEM((ROWS, 2 * WIDTH), f32), pltpu.VMEM((ROWS, WIDTH), f32),
            padded, frame, frame, frame, frame, frame, narrow, frame, narrow,
            share, share, share, pltpu.VMEM(totals_shape, bf16),
            dma((21,)), dma((2,)), dma((2,)), dma((2, CHUNKS)), dma((2, CHUNKS)),
            dma((10, CHUNKS)), dma((10, CHUNKS)),
            dma((2, SLABS, 2)), dma((2, SLABS, 6)), dma((2, 10)), dma((2, 10)), dma((14,)),
        ],
        compiler_params=pltpu.CompilerParams(
            collective_id=0, has_side_effects=True, vmem_limit_bytes=67043328
        ),
    )(*operands)


def scaled(total):
    count = lax.axis_size("dp") * lax.axis_size(("tx", "ty")) * ROWS
    value = total.astype(jnp.float32) * float(count) ** (-0.5)
    return value.reshape(128, total.shape[-1])


def shards(*operands):
    block_output, input_gradient, *totals = whole_step(*operands)
    conv_two, proj_two, conv_one, proj_one = (scaled(total) for total in totals)
    return (block_output, input_gradient, conv_one, proj_one, conv_two, proj_two)


def solution(mesh):
    return jax.shard_map(
        shards,
        mesh=mesh,
        in_specs=(P("dp", ("tx", "ty"), None), P(), P(), P(), P(), P("dp", ("tx", "ty"), None)),
        out_specs=(
            P("dp", ("tx", "ty"), None),
            P("dp", ("tx", "ty"), None),
            P("ty", None),
            P("ty", None),
            P("ty", None),
            P("ty", None),
        ),
        check_vma=False,
    )
```

```python
import jax
import jax.numpy as jnp
from jax import lax
from jax.experimental import pallas as pl
from jax.experimental.pallas import tpu as pltpu
from jax.sharding import PartitionSpec as P

NEAR = 64
ROWS = 384
WIDTH = 1024
CHUNKS = 3
CHUNK = ROWS // CHUNKS
TILE = 256
BROAD = 512
HALVES = 2
HALF_ROWS = ROWS // HALVES

MESH = pl.DeviceIdType.MESH
UNIT = 16
HALF = 2560
SLABS = 20
SLAB = 128
ORDERS = (
    (
        (0, 3, 5, 2, 4, 1),
        (1, 5, 2, 0, 3, 4),
        (2, 5, 4, 1, 0, 3),
        (3, 4, 0, 2, 1, 5),
        (4, 3, 1, 5, 0, 2),
        (5, 3, 1, 0, 4, 2),
        (0, 4, 5, 3, 2, 1),
        (1, 0, 2, 4, 5, 3),
        (2, 0, 3, 1, 4, 5),
        (3, 4, 5, 2, 1, 0),
        (4, 2, 3, 0, 5, 1),
        (5, 4, 2, 0, 1, 3),
        (0, 1, 3, 4, 2, 5),
        (1, 2, 5, 3, 4, 0),
        (2, 5, 0, 1, 3, 4),
        (3, 5, 1, 4, 2, 0),
        (4, 3, 0, 2, 5, 1),
        (5, 2, 4, 1, 0, 3),
        (0, 1, 3, 4, 2, 5),
        (1, 2, 4, 5, 3, 0),
    ),
    (
        (2, 4, 3, 1, 0, 5),
        (3, 4, 2, 1, 5, 0),
        (4, 5, 1, 0, 2, 3),
        (5, 0, 2, 4, 1, 3),
        (0, 1, 5, 4, 3, 2),
        (1, 2, 4, 3, 0, 5),
        (2, 1, 4, 3, 5, 0),
        (3, 0, 2, 4, 1, 5),
        (4, 2, 5, 1, 3, 0),
        (5, 0, 3, 1, 4, 2),
        (0, 3, 1, 5, 4, 2),
        (1, 3, 0, 5, 2, 4),
        (2, 0, 5, 3, 4, 1),
        (3, 5, 4, 2, 0, 1),
        (4, 1, 0, 2, 5, 3),
        (5, 1, 0, 4, 3, 2),
        (0, 5, 1, 3, 2, 4),
        (1, 5, 3, 2, 4, 0),
        (2, 4, 5, 0, 1, 3),
        (3, 4, 0, 2, 1, 5),
    ),
)


def place():
    dp, tx, ty = (lax.axis_index(name) for name in ("dp", "tx", "ty"))
    y_hi, core = lax.div(dp, 2), lax.rem(dp, 2)
    y_lo, z = lax.div(ty, 4), lax.rem(ty, 4)
    zh, xh = lax.div(z, 2), lax.div(tx, 2)
    bits = (
        zh,
        lax.rem(zh + z, 2),
        y_hi,
        lax.rem(y_hi + y_lo, 2),
        xh,
        lax.rem(xh + tx, 2),
    )
    peers = (
        {"ty": y_lo * 4 + 3 - z},
        {"ty": y_lo * 4 + z + 1 - 2 * lax.rem(z, 2)},
        {"dp": (1 - y_hi) * 2 + core, "ty": (1 - y_lo) * 4 + z},
        {"ty": (1 - y_lo) * 4 + z},
        {"tx": 3 - tx},
        {"tx": tx + 1 - 2 * lax.rem(tx, 2)},
    )
    other_core = {"dp": y_hi * 2 + 1 - core}
    far_y = {"dp": (1 - y_hi) * 2 + core}
    return bits, core, peers, other_core, far_y


def remote(source, target, send_sem, recv_sem, peer):
    return pltpu.make_async_remote_copy(
        src_ref=source,
        dst_ref=target,
        send_sem=send_sem,
        recv_sem=recv_sem,
        device_id=peer,
        device_id_type=MESH,
    )


def dot_nn(left, right):
    return jnp.dot(left, right, preferred_element_type=jnp.float32)


def dot_nt(left, right):
    return lax.dot_general(
        left, right, (((1,), (1,)), ((), ())), preferred_element_type=jnp.float32
    )


def dot_tn(left, right):
    return lax.dot_general(
        left, right, (((0,), (0,)), ((), ())), preferred_element_type=jnp.float32
    )


def step_kernel(
    frames, conv_1, proj_1, conv_2, proj_2, out_grad,
    out_frames, frame_grad, conv_total_2, proj_total_2, conv_total_1, proj_total_1,
    w1, w2, q1, q2, xs, mid, s2, t1, t2, g, gmid, gp1, gp2, slope_t, slope_g,
    tap_in, tap_out, near_tap, pre2, wide,
    xs_in, mid_in, s2_in, t1_in, t2_in, gp2_in, g_in, gp1_in, gm_in,
    acc2, got2, got1, full,
    ld_sem, near_send, near_recv, far_send, far_recv, ex_send, ex_recv,
    rs_send, rs_recv, ag_send, ag_recv, st_sem,
):
    bf16, f32 = jnp.bfloat16, jnp.float32
    bits, core, peers, other_core, far_y = place()
    tx, ty = lax.axis_index("tx"), lax.axis_index("ty")
    index = tx * 8 + ty
    after, before = lax.rem(index + 1, 32), lax.rem(index + 31, 32)
    next_peer = {"tx": lax.div(after, 8), "ty": lax.rem(after, 8)}
    prev_peer = {"tx": lax.div(before, 8), "ty": lax.rem(before, 8)}
    later_peer = {"tx": lax.rem(tx + 1, 4)}
    earlier_peer = {"tx": lax.rem(tx + 3, 4)}
    first_shard, last_shard = index == 0, index == 31

    def load(index, source, target):
        return pltpu.make_async_copy(source, target, ld_sem.at[index])

    def columns(start):
        return pl.ds(pl.multiple_of(start, TILE), TILE)

    def broad(start):
        return pl.ds(pl.multiple_of(start, BROAD), BROAD)

    def conv_loads(j):
        return [
            load(
                4 * j + part,
                conv_1.at[:, pl.ds(part * WIDTH + j * BROAD, BROAD)],
                w1.at[:, pl.ds(part * WIDTH + j * BROAD, BROAD)],
            )
            for part in range(4)
        ]

    loads = {"x": load(16, frames.at[0], xs.at[pl.ds(NEAR, ROWS), :])}
    loads["q1"] = load(17, proj_1, q1)
    loads["w2"] = load(18, conv_2, w2)
    loads["g"] = load(19, out_grad.at[0], g)
    loads["q2"] = load(20, proj_2, q2)
    barrier = pltpu.get_barrier_semaphore()
    for peer in peers + (other_core, far_y, next_peer, prev_peer):
        pl.semaphore_signal(barrier, inc=1, device_id=peer, device_id_type=MESH)
    loads["x"].start()
    pl.semaphore_wait(barrier, 10)
    near_forward = remote(
        frames.at[0, pl.ds(ROWS - NEAR, NEAR), :], xs.at[pl.ds(0, NEAR), :],
        near_send.at[0], near_recv.at[0], next_peer,
    )
    near_forward.start()
    for j in range(2):
        for copy in conv_loads(j):
            copy.start()
    loads["q1"].start()

    def half(ref, which, width):
        return ref.at[:, pl.ds(pl.multiple_of(which * width, width), width)]

    def half_rows(ref, which, width, rows):
        return ref.at[rows, pl.ds(pl.multiple_of(which * width, width), width)]

    def swap(item, part, source, target):
        return remote(
            source, target, ex_send.at[item, part], ex_recv.at[item, part], other_core
        )

    every = slice(None)
    top = pl.ds(0, NEAR)
    parts = [pl.ds(c * CHUNK, CHUNK) for c in range(CHUNKS)]
    halves = [pl.ds(c * HALF_ROWS, HALF_ROWS) for c in range(HALVES)]
    swaps = {
        "x": [swap(0, 0, frames.at[0], xs_in.at[pl.ds(NEAR, ROWS), :])],
        "halo": [swap(1, 0, xs.at[top, :], xs_in.at[top, :])],
        "g": [swap(2, 0, half(out_grad.at[0], 1 - core, 512), g_in)],
    }
    for item, (name, source, target) in enumerate(
        (("t1", t1, t1_in), ("mid", mid, mid_in), ("s2", s2, s2_in), ("t2", t2, t2_in)), 3
    ):
        swaps[name] = [
            swap(item, c, source.at[rows, :], target.at[rows, :])
            for c, rows in enumerate(parts)
        ]
    for item, (name, source, target, width, pieces) in enumerate(
        (
            ("gp2", gp2, gp2_in, 1024, parts),
            ("gp1", gp1, gp1_in, 1024, halves),
            ("gm", gmid, gm_in, 512, halves),
        ),
        7,
    ):
        swaps[name] = [
            swap(item, c, half_rows(source, 1 - core, width, rows), target.at[rows, :])
            for c, rows in enumerate(pieces)
        ]

    near_back = remote(
        tap_out.at[top, :], near_tap, near_send.at[1], near_recv.at[1], prev_peer
    )
    far_forward = [
        remote(
            mid.at[rows, :], s2.at[rows, :], far_send.at[0, c], far_recv.at[0, c], later_peer
        )
        for c, rows in enumerate(parts)
    ]
    far_back = [
        remote(
            tap_out.at[rows, :], tap_in.at[rows, :],
            far_send.at[1, c], far_recv.at[1, c], earlier_peer,
        )
        for c, rows in enumerate(parts)
    ]

    loads["x"].wait()

    def share_inputs():
        swaps["x"][0].start()
        swaps["g"][0].start()

    def take_halo():
        near_forward.wait_recv()

        @pl.when(first_shard)
        def _():
            xs[0:NEAR, :] = jnp.zeros((NEAR, WIDTH), bf16)

        swaps["halo"][0].start()

    def tiles(count, body):
        def step(j, carry):
            body(j)
            return carry

        lax.fori_loop(0, count, step, 0)

    def first_forward(c):
        low = c * CHUNK
        rows = slice(low, low + CHUNK)
        moved = slice(NEAR + low, NEAR + low + CHUNK)

        def gate_tile(j):
            old, now = xs[rows, :], xs[moved, :]
            start = j * BROAD
            a = dot_nn(old, w1[:, broad(start)]) + dot_nn(
                now, w1[:, broad(2 * WIDTH + start)]
            )
            v = dot_nn(old, w1[:, broad(WIDTH + start)]) + dot_nn(
                now, w1[:, broad(3 * WIDTH + start)]
            )
            th, gt = jnp.tanh(a), jax.nn.sigmoid(v)
            t1[rows, broad(start)] = (th * gt).astype(bf16)
            slope_t[rows, broad(start)] = (gt * (1.0 - th * th)).astype(bf16)
            slope_g[rows, broad(start)] = (th * gt * (1.0 - gt)).astype(bf16)

        if c == 1:
            for j in range(2):
                for copy in conv_loads(j):
                    copy.wait()
                gate_tile(j)
                if j == 0:
                    for name in ("w2", "g", "q2"):
                        loads[name].start()
            loads["q1"].wait()
            share_inputs()
        else:
            if c == 0:
                take_halo()
            tiles(2, gate_tile)
        swaps["t1"][c].start()

        def out_tile(j):
            value = dot_nn(t1[rows, :], q1[:, broad(j * BROAD)])
            value = value + xs[moved, broad(j * BROAD)].astype(f32)
            mid[rows, broad(j * BROAD)] = value.astype(bf16)

        tiles(2, out_tile)
        far_forward[c].start()
        swaps["mid"][c].start()

    turns = (1, 2, 0)
    for c in turns:
        first_forward(c)

    loads["w2"].wait()

    def pre_tile(j):
        pre2[:, broad(j * BROAD)] = dot_nn(mid[...], w2[:, broad(2 * WIDTH + j * BROAD)])

    tiles(4, pre_tile)
    loads["g"].wait()
    loads["q2"].wait()

    def gated_grad_tile(j):
        wide[:, broad(j * BROAD)] = dot_nt(g[...], q2[broad(j * BROAD), :])

    tiles(2, gated_grad_tile)

    def second_block(c):
        low = c * CHUNK
        rows = slice(low, low + CHUNK)
        far_forward[c].wait_recv()

        @pl.when(tx == 0)
        def _():
            s2[rows, :] = jnp.zeros((CHUNK, WIDTH), bf16)

        swaps["s2"][c].start()

        def gate_tile(j):
            old = s2[rows, :]
            here, there = broad(j * BROAD), broad(WIDTH + j * BROAD)
            a = dot_nn(old, w2[:, here]) + pre2[rows, here]
            v = dot_nn(old, w2[:, there]) + pre2[rows, there]
            th, gt = jnp.tanh(a), jax.nn.sigmoid(v)
            t2[rows, here] = (th * gt).astype(bf16)
            grad = wide[rows, here] * gt
            gp2[rows, here] = (grad * (1.0 - th * th)).astype(bf16)
            gp2[rows, there] = (grad * th * (1.0 - gt)).astype(bf16)

        tiles(2, gate_tile)
        swaps["t2"][c].start()
        swaps["gp2"][c].start()

        def tap_tile(j):
            value = dot_nt(gp2[rows, :], w2[broad(j * BROAD), 0 : 2 * WIDTH])
            tap_out[rows, broad(j * BROAD)] = value.astype(bf16)

        tiles(2, tap_tile)
        far_back[c].start()

    for c in turns:
        second_block(c)

    def units(start, count):
        return pl.ds(pl.multiple_of(start * UNIT, UNIT), count * UNIT)

    def ours(b, slab, rows):
        return (acc2, w2)[b].at[rows, slab * SLAB : slab * SLAB + SLAB]

    def theirs(b, slab, rows):
        return (got2, got1)[b].at[rows, slab * SLAB : slab * SLAB + SLAB]

    def weight_products(b, part):
        if b == 0:
            lefts = ((s2, 0, s2_in), (mid, 0, mid_in), (t2, 0, t2_in))
            own_p, own_g = half(gp2, core, 1024), half(g, core, 512)
            pre_in, grad_in = gp2_in, g_in
        else:
            lefts = ((xs, 0, xs_in), (xs, NEAR, xs_in), (t1, 0, t1_in))
            own_p, own_g = half(gp1, core, 1024), half(gmid, core, 512)
            pre_in, grad_in = gp1_in, gm_in
        def product_tile(m):
            own, low, partner = lefts[part]
            span = slice(low, low + ROWS)
            left = jnp.concatenate(
                [own[span, columns(m * TILE)], partner[span, columns(m * TILE)]], 0
            )
            for piece in range(2 if part < 2 else 1):
                lo = piece * 512
                if part < 2:
                    right = jnp.concatenate(
                        [own_p[:, lo : lo + 512], pre_in[:, lo : lo + 512]], 0
                    )
                else:
                    right = jnp.concatenate([own_g[...], grad_in[...]], 0)
                product = dot_tn(left, right).astype(bf16)
                first = part * 1024 + lo
                for row in range(16):
                    block = 2 * m + row // 8
                    y_lo, z = lax.div(block, 4), lax.rem(block, 4)
                    zh = lax.div(z, 2)
                    side = (row // 4) % 2
                    moving = {0: zh, 1: lax.rem(zh + z, 2), 3: lax.rem(side + y_lo, 2)}
                    fixed = {2: side, 4: (row // 2) % 2, 5: row % 2}
                    for local in range(512 // SLAB):
                        slab = first // SLAB + local
                        weight = {
                            dim: 2 ** (5 - step) for step, dim in enumerate(ORDERS[b][slab])
                        }
                        spot = sum(moving[dim] * weight[dim] for dim in moving)
                        spot = spot + sum(fixed[dim] * weight[dim] for dim in fixed)
                        ours(b, slab, units(spot, 1))[...] = product[
                            row * 16 : row * 16 + 16, local * SLAB : local * SLAB + SLAB
                        ]

        tiles(4, product_tile)

    def ranges(b, slab, step):
        base = 0
        for earlier, dim in enumerate(ORDERS[b][slab][:step]):
            base = base + bits[dim] * 2 ** (5 - earlier)
        count = 2 ** (5 - step)
        mine = bits[ORDERS[b][slab][step]]
        return base + mine * count, base + (1 - mine) * count, count

    def reduce_copy(b, slab, step, landing):
        keep, give, count = ranges(b, slab, step)
        return remote(
            ours(b, slab, units(give, count)),
            theirs(b, slab, units(keep if landing else give, count)),
            rs_send.at[b, slab, step % 2], rs_recv.at[b, slab, step],
            peers[ORDERS[b][slab][step]],
        )

    yh, xh, xq = bits[2], bits[4], bits[5]

    def fold(b, slab, step):
        keep, give, count = ranges(b, slab, step)
        chunk = min(count, 32)

        def total(i):
            here = ours(b, slab, units(keep + i * chunk, chunk))[...]
            return here + theirs(b, slab, units(give + i * chunk, chunk))[...]

        if step == 5:
            full[b, core, yh, xh, xq, :, slab * SLAB : slab * SLAB + SLAB] = total(0)
            return
        for i in range(count // chunk):
            ours(b, slab, units(keep + i * chunk, chunk))[...] = total(i)

    def slabs_of(part):
        return range(8 * part, min(8 * part + 8, SLABS))

    def advance(b, step, slabs=range(SLABS)):
        for slab in slabs:
            reduce_copy(b, slab, step, False).wait_recv()
            fold(b, slab, step)
            if step < 5:
                reduce_copy(b, slab, step + 1, True).start()
        for slab in slabs:
            reduce_copy(b, slab, step, True).wait_send()

    def begin_reduce(b, part):
        for slab in slabs_of(part):
            reduce_copy(b, slab, 0, True).start()

    for name in ("mid", "s2", "t2", "gp2", "g"):
        for copy in swaps[name]:
            copy.wait_recv()
    for part in range(3):
        weight_products(0, part)
        begin_reduce(0, part)

    def current_tile(j):
        value = dot_nt(gp2[...], w2[broad(j * BROAD), 2 * WIDTH : 4 * WIDTH])
        wide[:, broad(j * BROAD)] = value + g[:, broad(j * BROAD)].astype(f32)

    tiles(2, current_tile)

    def first_backward(c):
        low = c * HALF_ROWS
        rows = slice(low, low + HALF_ROWS)
        tap = tap_in[rows, :].astype(f32)
        total = wide[rows, :] + jnp.where(tx == 3, 0.0, tap)
        gmid[rows, :] = total.astype(bf16)
        swaps["gm"][c].start()

        def slope_tile(j):
            here, there = broad(j * BROAD), broad(WIDTH + j * BROAD)
            grad = dot_nt(gmid[rows, :], q1[here, :])
            gp1[rows, here] = (grad * slope_t[rows, here].astype(f32)).astype(bf16)
            gp1[rows, there] = (grad * slope_g[rows, here].astype(f32)).astype(bf16)

        tiles(2, slope_tile)
        swaps["gp1"][c].start()

    for copy in far_back:
        copy.wait_recv()
    for c in range(HALVES):
        first_backward(c)
    for copy in far_forward + swaps["mid"]:
        copy.wait_send()

    def second_out_tile(j):
        value = dot_nn(t2[...], q2[:, broad(j * BROAD)])
        mid[:, broad(j * BROAD)] = (value + mid[:, broad(j * BROAD)].astype(f32)).astype(bf16)

    tiles(2, second_out_tile)
    store_out = pltpu.make_async_copy(mid, out_frames.at[0], st_sem.at[0])
    store_out.start()
    for name in ("x", "halo", "t1", "gp1", "gm"):
        for copy in swaps[name]:
            copy.wait_recv()
    for part in range(3):
        weight_products(1, part)
        begin_reduce(1, part)
    advance(0, 0)

    for copy in far_back:
        copy.wait_send()

    def first_tap_tile(j):
        value = dot_nt(gp1[...], w1[broad(j * BROAD), 0 : 2 * WIDTH])
        tap_out[:, broad(j * BROAD)] = value.astype(bf16)

    tiles(2, first_tap_tile)
    near_back.start()

    def first_current_tile(j):
        value = dot_nt(gp1[...], w1[broad(j * BROAD), 2 * WIDTH : 4 * WIDTH])
        pre2[:, broad(j * BROAD)] = value + gmid[:, broad(j * BROAD)].astype(f32)

    tiles(2, first_current_tile)
    advance(1, 0)
    advance(0, 1)
    near_back.wait_recv()
    for copy in swaps["gm"]:
        copy.wait_send()
    body_rows = ROWS - NEAR
    gmid[0:body_rows, :] = (
        pre2[0:body_rows, 0:WIDTH] + tap_out[NEAR:ROWS, :].astype(f32)
    ).astype(bf16)
    edge = jnp.where(last_shard, 0.0, near_tap[...].astype(f32))
    gmid[body_rows:ROWS, :] = (pre2[body_rows:ROWS, 0:WIDTH] + edge).astype(bf16)
    store_grad = pltpu.make_async_copy(gmid, frame_grad.at[0], st_sem.at[1])
    store_grad.start()

    left, right = slice(0, HALF // 2), slice(HALF // 2, HALF)

    def gather_copy(b, index, where, target):
        ref = full.at[(b, core) + where]
        return remote(ref, ref, ag_send.at[b, index], ag_recv.at[b, index], target)

    places = (
        ((yh, xh, xq), far_y),
        ((every, xh, xq, every, left), peers[5]),
        ((every, xh, xq, every, right), peers[4]),
        ((every, xh, every, every, left), peers[4]),
        ((every, every, xq, every, right), peers[5]),
        ((every, xh, xq), other_core),
        ((every, xh, 1 - xq, every, left), other_core),
        ((every, 1 - xh, xq, every, right), other_core),
        ((every, 1 - xh, every, every, left), other_core),
        ((every, every, 1 - xq, every, right), other_core),
    )

    def gather(b, index):
        return gather_copy(b, index, *places[index])

    def stores(b):
        conv, proj = ((conv_total_2, proj_total_2), (conv_total_1, proj_total_1))[b]
        copies = []
        for k in (core, 1 - core):
            moves = (
                (conv, k * 1024, 0, 1024),
                (conv, 2048 + k * 1024, 1024, 1024),
                (proj, k * 512, 2048, 512),
            )
            for target, to, start, width in moves:
                copies.append(
                    pltpu.make_async_copy(
                        full.at[b, k, :, :, :, :, start : start + width],
                        target.at[:, :, :, :, pl.ds(pl.multiple_of(to, width), width)],
                        st_sem.at[2 + b * 6 + len(copies)],
                    )
                )
        return copies

    def gather_stage(b, stage):
        waits = ((), (0,), (1, 2), (3, 4), (5, 6, 7, 8, 9))[stage]
        starts = ((0,), (1, 2, 5), (3, 4, 6, 7), (8, 9), ())[stage]
        for index in waits:
            gather(b, index).wait_recv()
        for index in starts:
            gather(b, index).start()
        if stage >= 3:
            for copy in stores(b)[3 * stage - 9 : 3 * stage - 6]:
                copy.start()

    for step in range(1, 5):
        advance(1, step)
        advance(0, step + 1)
    gather_stage(0, 0)
    advance(1, 5)
    gather_stage(1, 0)
    gather_stage(0, 1)
    gather_stage(1, 1)
    gather_stage(0, 2)
    gather_stage(1, 2)
    gather_stage(0, 3)
    near_forward.wait_send()
    near_back.wait_send()
    for name, copies in swaps.items():
        if name not in ("mid", "gm"):
            for copy in copies:
                copy.wait_send()
    store_out.wait()
    store_grad.wait()
    gather_stage(0, 4)
    gather_stage(1, 3)
    gather_stage(1, 4)

    for b in range(2):
        for index in range(10):
            gather(b, index).wait_send()
        for copy in stores(b):
            copy.wait()


def whole_step(*operands):
    anywhere = pl.BlockSpec(memory_space=pl.ANY)
    bf16, f32 = jnp.bfloat16, jnp.float32
    frame_shape = jax.ShapeDtypeStruct((1, ROWS, WIDTH), bf16)
    totals_shape = (2, 2, 2, 2, 2, UNIT, HALF)
    conv_shape = jax.ShapeDtypeStruct((2, 2, 2, UNIT, 4 * WIDTH), bf16)
    proj_shape = jax.ShapeDtypeStruct((2, 2, 2, UNIT, WIDTH), bf16)
    frame = pltpu.VMEM((ROWS, WIDTH), bf16)
    double = pltpu.VMEM((ROWS, 2 * WIDTH), bf16)
    narrow = pltpu.VMEM((ROWS, WIDTH // 2), bf16)
    weight = pltpu.VMEM((WIDTH, 4 * WIDTH), bf16)
    square = pltpu.VMEM((WIDTH, WIDTH), bf16)
    padded = pltpu.VMEM((ROWS + NEAR, WIDTH), bf16)
    share = pltpu.VMEM((WIDTH, HALF), bf16)
    dma = pltpu.SemaphoreType.DMA
    return pl.pallas_call(
        step_kernel,
        out_shape=[frame_shape, frame_shape] + [conv_shape, proj_shape] * 2,
        in_specs=[anywhere] * 6,
        out_specs=[anywhere] * 6,
        scratch_shapes=[
            weight, weight, square, square,
            padded, frame, frame, frame, frame, frame, frame,
            double, double, frame, frame,
            frame, frame, pltpu.VMEM((NEAR, WIDTH), bf16),
            pltpu.VMEM((ROWS, 2 * WIDTH), f32), pltpu.VMEM((ROWS, WIDTH), f32),
            padded, frame, frame, frame, frame, frame, narrow, frame, narrow,
            share, share, share, pltpu.VMEM(totals_shape, bf16),
            dma((21,)), dma((2,)), dma((2,)), dma((2, CHUNKS)), dma((2, CHUNKS)),
            dma((10, CHUNKS)), dma((10, CHUNKS)),
            dma((2, SLABS, 2)), dma((2, SLABS, 6)), dma((2, 10)), dma((2, 10)), dma((14,)),
        ],
        compiler_params=pltpu.CompilerParams(
            collective_id=0, has_side_effects=True, vmem_limit_bytes=67043328
        ),
    )(*operands)


def scaled(total):
    count = lax.axis_size("dp") * lax.axis_size(("tx", "ty")) * ROWS
    value = total.astype(jnp.float32) * float(count) ** (-0.5)
    return value.reshape(128, total.shape[-1])


def shards(*operands):
    block_output, input_gradient, *totals = whole_step(*operands)
    conv_two, proj_two, conv_one, proj_one = (scaled(total) for total in totals)
    return (block_output, input_gradient, conv_one, proj_one, conv_two, proj_two)


def solution(mesh):
    return jax.shard_map(
        shards,
        mesh=mesh,
        in_specs=(P("dp", ("tx", "ty"), None), P(), P(), P(), P(), P("dp", ("tx", "ty"), None)),
        out_specs=(
            P("dp", ("tx", "ty"), None),
            P("dp", ("tx", "ty"), None),
            P("ty", None),
            P("ty", None),
            P("ty", None),
            P("ty", None),
        ),
        check_vma=False,
    )
```

```python
import jax
import jax.numpy as jnp
from jax import lax
from jax.experimental import pallas as pl
from jax.experimental.pallas import tpu as pltpu
from jax.sharding import PartitionSpec as P

NEAR = 64
ROWS = 384
WIDTH = 1024
CHUNKS = 3
CHUNK = ROWS // CHUNKS
TILE = 256
BROAD = 512
HALVES = 2
HALF_ROWS = ROWS // HALVES

MESH = pl.DeviceIdType.MESH
UNIT = 16
HALF = 2560
SLABS = 20
SLAB = 128
ORDERS = (
    (
        (0, 3, 5, 2, 4, 1),
        (1, 5, 2, 0, 3, 4),
        (2, 5, 4, 1, 0, 3),
        (3, 4, 0, 2, 1, 5),
        (4, 3, 1, 5, 0, 2),
        (5, 3, 1, 0, 4, 2),
        (0, 4, 5, 3, 2, 1),
        (1, 0, 2, 4, 5, 3),
        (2, 0, 3, 1, 4, 5),
        (3, 4, 5, 2, 1, 0),
        (4, 2, 3, 0, 5, 1),
        (5, 4, 2, 0, 1, 3),
        (0, 1, 3, 4, 2, 5),
        (1, 2, 5, 3, 4, 0),
        (2, 5, 0, 1, 3, 4),
        (3, 5, 1, 4, 2, 0),
        (4, 3, 0, 2, 5, 1),
        (5, 2, 4, 1, 0, 3),
        (0, 1, 3, 4, 2, 5),
        (1, 2, 4, 5, 3, 0),
    ),
    (
        (2, 4, 3, 1, 0, 5),
        (3, 4, 2, 1, 5, 0),
        (4, 5, 1, 0, 2, 3),
        (5, 0, 2, 4, 1, 3),
        (0, 1, 5, 4, 3, 2),
        (1, 2, 4, 3, 0, 5),
        (2, 1, 4, 3, 5, 0),
        (3, 0, 2, 4, 1, 5),
        (4, 2, 5, 1, 3, 0),
        (5, 0, 3, 1, 4, 2),
        (0, 3, 1, 5, 4, 2),
        (1, 3, 0, 5, 2, 4),
        (2, 0, 5, 3, 4, 1),
        (3, 5, 4, 2, 0, 1),
        (4, 1, 0, 2, 5, 3),
        (5, 1, 0, 4, 3, 2),
        (0, 5, 1, 3, 2, 4),
        (1, 5, 3, 2, 4, 0),
        (2, 4, 5, 0, 1, 3),
        (3, 4, 0, 2, 1, 5),
    ),
)


def place():
    dp, tx, ty = (lax.axis_index(name) for name in ("dp", "tx", "ty"))
    y_hi, core = lax.div(dp, 2), lax.rem(dp, 2)
    y_lo, z = lax.div(ty, 4), lax.rem(ty, 4)
    zh, xh = lax.div(z, 2), lax.div(tx, 2)
    bits = (
        zh,
        lax.rem(zh + z, 2),
        y_hi,
        lax.rem(y_hi + y_lo, 2),
        xh,
        lax.rem(xh + tx, 2),
    )
    peers = (
        {"ty": y_lo * 4 + 3 - z},
        {"ty": y_lo * 4 + z + 1 - 2 * lax.rem(z, 2)},
        {"dp": (1 - y_hi) * 2 + core, "ty": (1 - y_lo) * 4 + z},
        {"ty": (1 - y_lo) * 4 + z},
        {"tx": 3 - tx},
        {"tx": tx + 1 - 2 * lax.rem(tx, 2)},
    )
    other_core = {"dp": y_hi * 2 + 1 - core}
    far_y = {"dp": (1 - y_hi) * 2 + core}
    return bits, core, peers, other_core, far_y


def remote(source, target, send_sem, recv_sem, peer):
    return pltpu.make_async_remote_copy(
        src_ref=source,
        dst_ref=target,
        send_sem=send_sem,
        recv_sem=recv_sem,
        device_id=peer,
        device_id_type=MESH,
    )


def dot_nn(left, right):
    return jnp.dot(left, right, preferred_element_type=jnp.float32)


def dot_nt(left, right):
    return lax.dot_general(
        left, right, (((1,), (1,)), ((), ())), preferred_element_type=jnp.float32
    )


def dot_tn(left, right):
    return lax.dot_general(
        left, right, (((0,), (0,)), ((), ())), preferred_element_type=jnp.float32
    )


def step_kernel(
    frames, conv_1, proj_1, conv_2, proj_2, out_grad,
    out_frames, frame_grad, conv_total_2, proj_total_2, conv_total_1, proj_total_1,
    w1, w2, q1, q2, xs, mid, s2, t1, t2, g, gmid, gp1, gp2, slope_t, slope_g,
    tap_in, tap_out, near_tap, pre2, wide,
    xs_in, mid_in, s2_in, t1_in, t2_in, gp2_in, g_in, gp1_in, gm_in,
    acc2, got2, got1, full,
    ld_sem, near_send, near_recv, far_send, far_recv, ex_send, ex_recv,
    rs_send, rs_recv, ag_send, ag_recv, st_sem,
):
    bf16, f32 = jnp.bfloat16, jnp.float32
    bits, core, peers, other_core, far_y = place()
    tx, ty = lax.axis_index("tx"), lax.axis_index("ty")
    index = tx * 8 + ty
    after, before = lax.rem(index + 1, 32), lax.rem(index + 31, 32)
    next_peer = {"tx": lax.div(after, 8), "ty": lax.rem(after, 8)}
    prev_peer = {"tx": lax.div(before, 8), "ty": lax.rem(before, 8)}
    later_peer = {"tx": lax.rem(tx + 1, 4)}
    earlier_peer = {"tx": lax.rem(tx + 3, 4)}
    first_shard, last_shard = index == 0, index == 31

    def load(index, source, target):
        return pltpu.make_async_copy(source, target, ld_sem.at[index])

    def columns(start):
        return pl.ds(pl.multiple_of(start, TILE), TILE)

    def broad(start):
        return pl.ds(pl.multiple_of(start, BROAD), BROAD)

    def conv_loads(j):
        return [
            load(
                4 * j + part,
                conv_1.at[:, pl.ds(part * WIDTH + j * BROAD, BROAD)],
                w1.at[:, pl.ds(part * WIDTH + j * BROAD, BROAD)],
            )
            for part in range(4)
        ]

    loads = {"x": load(16, frames.at[0], xs.at[pl.ds(NEAR, ROWS), :])}
    loads["q1"] = load(17, proj_1, q1)
    loads["w2"] = load(18, conv_2, w2)
    loads["g"] = load(19, out_grad.at[0], g)
    loads["q2"] = load(20, proj_2, q2)
    barrier = pltpu.get_barrier_semaphore()
    for peer in peers + (other_core, far_y, next_peer, prev_peer):
        pl.semaphore_signal(barrier, inc=1, device_id=peer, device_id_type=MESH)
    loads["x"].start()
    pl.semaphore_wait(barrier, 10)
    near_forward = remote(
        frames.at[0, pl.ds(ROWS - NEAR, NEAR), :], xs.at[pl.ds(0, NEAR), :],
        near_send.at[0], near_recv.at[0], next_peer,
    )
    near_forward.start()
    for j in range(2):
        for copy in conv_loads(j):
            copy.start()
    loads["q1"].start()

    def half(ref, which, width):
        return ref.at[:, pl.ds(pl.multiple_of(which * width, width), width)]

    def half_rows(ref, which, width, rows):
        return ref.at[rows, pl.ds(pl.multiple_of(which * width, width), width)]

    def swap(item, part, source, target):
        return remote(
            source, target, ex_send.at[item, part], ex_recv.at[item, part], other_core
        )

    every = slice(None)
    top = pl.ds(0, NEAR)
    parts = [pl.ds(c * CHUNK, CHUNK) for c in range(CHUNKS)]
    halves = [pl.ds(c * HALF_ROWS, HALF_ROWS) for c in range(HALVES)]
    swaps = {
        "x": [swap(0, 0, frames.at[0], xs_in.at[pl.ds(NEAR, ROWS), :])],
        "halo": [swap(1, 0, xs.at[top, :], xs_in.at[top, :])],
        "g": [swap(2, 0, half(out_grad.at[0], 1 - core, 512), g_in)],
    }
    for item, (name, source, target) in enumerate(
        (("t1", t1, t1_in), ("mid", mid, mid_in), ("s2", s2, s2_in), ("t2", t2, t2_in)), 3
    ):
        swaps[name] = [
            swap(item, c, source.at[rows, :], target.at[rows, :])
            for c, rows in enumerate(parts)
        ]
    for item, (name, source, target, width, pieces) in enumerate(
        (
            ("gp2", gp2, gp2_in, 1024, parts),
            ("gp1", gp1, gp1_in, 1024, halves),
            ("gm", gmid, gm_in, 512, halves),
        ),
        7,
    ):
        swaps[name] = [
            swap(item, c, half_rows(source, 1 - core, width, rows), target.at[rows, :])
            for c, rows in enumerate(pieces)
        ]

    near_back = remote(
        tap_out.at[top, :], near_tap, near_send.at[1], near_recv.at[1], prev_peer
    )
    far_forward = [
        remote(
            mid.at[rows, :], s2.at[rows, :], far_send.at[0, c], far_recv.at[0, c], later_peer
        )
        for c, rows in enumerate(parts)
    ]
    far_back = [
        remote(
            tap_out.at[rows, :], tap_in.at[rows, :],
            far_send.at[1, c], far_recv.at[1, c], earlier_peer,
        )
        for c, rows in enumerate(parts)
    ]

    loads["x"].wait()

    def share_inputs():
        swaps["x"][0].start()
        swaps["g"][0].start()

    def take_halo():
        near_forward.wait_recv()

        @pl.when(first_shard)
        def _():
            xs[0:NEAR, :] = jnp.zeros((NEAR, WIDTH), bf16)

        swaps["halo"][0].start()

    def tiles(count, body):
        def step(j, carry):
            body(j)
            return carry

        lax.fori_loop(0, count, step, 0)

    def first_forward(c):
        low = c * CHUNK
        rows = slice(low, low + CHUNK)
        moved = slice(NEAR + low, NEAR + low + CHUNK)

        def gate_tile(j):
            old, now = xs[rows, :], xs[moved, :]
            start = j * BROAD
            a = dot_nn(old, w1[:, broad(start)]) + dot_nn(
                now, w1[:, broad(2 * WIDTH + start)]
            )
            v = dot_nn(old, w1[:, broad(WIDTH + start)]) + dot_nn(
                now, w1[:, broad(3 * WIDTH + start)]
            )
            th, gt = jnp.tanh(a), jax.nn.sigmoid(v)
            t1[rows, broad(start)] = (th * gt).astype(bf16)
            slope_t[rows, broad(start)] = (gt * (1.0 - th * th)).astype(bf16)
            slope_g[rows, broad(start)] = (th * gt * (1.0 - gt)).astype(bf16)

        if c == 1:
            for j in range(2):
                for copy in conv_loads(j):
                    copy.wait()
                gate_tile(j)
                if j == 0:
                    for name in ("w2", "g", "q2"):
                        loads[name].start()
            loads["q1"].wait()
            share_inputs()
        else:
            if c == 0:
                take_halo()
            tiles(2, gate_tile)
        swaps["t1"][c].start()

        def out_tile(j):
            value = dot_nn(t1[rows, :], q1[:, broad(j * BROAD)])
            value = value + xs[moved, broad(j * BROAD)].astype(f32)
            mid[rows, broad(j * BROAD)] = value.astype(bf16)

        tiles(2, out_tile)
        far_forward[c].start()
        swaps["mid"][c].start()

    turns = (1, 2, 0)
    for c in turns:
        first_forward(c)

    loads["w2"].wait()

    def pre_tile(j):
        pre2[:, broad(j * BROAD)] = dot_nn(mid[...], w2[:, broad(2 * WIDTH + j * BROAD)])

    tiles(4, pre_tile)
    loads["g"].wait()
    loads["q2"].wait()

    def gated_grad_tile(j):
        wide[:, broad(j * BROAD)] = dot_nt(g[...], q2[broad(j * BROAD), :])

    tiles(2, gated_grad_tile)

    def second_block(c):
        low = c * CHUNK
        rows = slice(low, low + CHUNK)
        far_forward[c].wait_recv()

        @pl.when(tx == 0)
        def _():
            s2[rows, :] = jnp.zeros((CHUNK, WIDTH), bf16)

        swaps["s2"][c].start()

        def gate_tile(j):
            old = s2[rows, :]
            here, there = broad(j * BROAD), broad(WIDTH + j * BROAD)
            a = dot_nn(old, w2[:, here]) + pre2[rows, here]
            v = dot_nn(old, w2[:, there]) + pre2[rows, there]
            th, gt = jnp.tanh(a), jax.nn.sigmoid(v)
            t2[rows, here] = (th * gt).astype(bf16)
            grad = wide[rows, here] * gt
            gp2[rows, here] = (grad * (1.0 - th * th)).astype(bf16)
            gp2[rows, there] = (grad * th * (1.0 - gt)).astype(bf16)

        tiles(2, gate_tile)
        swaps["t2"][c].start()
        swaps["gp2"][c].start()

        def tap_tile(j):
            value = dot_nt(gp2[rows, :], w2[broad(j * BROAD), 0 : 2 * WIDTH])
            tap_out[rows, broad(j * BROAD)] = value.astype(bf16)

        tiles(2, tap_tile)
        far_back[c].start()

    for c in turns:
        second_block(c)

    def units(start, count):
        return pl.ds(pl.multiple_of(start * UNIT, UNIT), count * UNIT)

    def ours(b, slab, rows):
        return (acc2, w2)[b].at[rows, slab * SLAB : slab * SLAB + SLAB]

    def theirs(b, slab, rows):
        return (got2, got1)[b].at[rows, slab * SLAB : slab * SLAB + SLAB]

    def weight_products(b, part):
        if b == 0:
            lefts = ((s2, 0, s2_in), (mid, 0, mid_in), (t2, 0, t2_in))
            own_p, own_g = half(gp2, core, 1024), half(g, core, 512)
            pre_in, grad_in = gp2_in, g_in
        else:
            lefts = ((xs, 0, xs_in), (xs, NEAR, xs_in), (t1, 0, t1_in))
            own_p, own_g = half(gp1, core, 1024), half(gmid, core, 512)
            pre_in, grad_in = gp1_in, gm_in
        def product_tile(m):
            own, low, partner = lefts[part]
            span = slice(low, low + ROWS)
            left = jnp.concatenate(
                [own[span, columns(m * TILE)], partner[span, columns(m * TILE)]], 0
            )
            for piece in range(2 if part < 2 else 1):
                lo = piece * 512
                if part < 2:
                    right = jnp.concatenate(
                        [own_p[:, lo : lo + 512], pre_in[:, lo : lo + 512]], 0
                    )
                else:
                    right = jnp.concatenate([own_g[...], grad_in[...]], 0)
                product = dot_tn(left, right).astype(bf16)
                first = part * 1024 + lo
                for row in range(16):
                    block = 2 * m + row // 8
                    y_lo, z = lax.div(block, 4), lax.rem(block, 4)
                    zh = lax.div(z, 2)
                    side = (row // 4) % 2
                    moving = {0: zh, 1: lax.rem(zh + z, 2), 3: lax.rem(side + y_lo, 2)}
                    fixed = {2: side, 4: (row // 2) % 2, 5: row % 2}
                    for local in range(512 // SLAB):
                        slab = first // SLAB + local
                        weight = {
                            dim: 2 ** (5 - step) for step, dim in enumerate(ORDERS[b][slab])
                        }
                        spot = sum(moving[dim] * weight[dim] for dim in moving)
                        spot = spot + sum(fixed[dim] * weight[dim] for dim in fixed)
                        ours(b, slab, units(spot, 1))[...] = product[
                            row * 16 : row * 16 + 16, local * SLAB : local * SLAB + SLAB
                        ]

        tiles(4, product_tile)

    def ranges(b, slab, step):
        base = 0
        for earlier, dim in enumerate(ORDERS[b][slab][:step]):
            base = base + bits[dim] * 2 ** (5 - earlier)
        count = 2 ** (5 - step)
        mine = bits[ORDERS[b][slab][step]]
        return base + mine * count, base + (1 - mine) * count, count

    def reduce_copy(b, slab, step, landing):
        keep, give, count = ranges(b, slab, step)
        return remote(
            ours(b, slab, units(give, count)),
            theirs(b, slab, units(keep if landing else give, count)),
            rs_send.at[b, step % 2],
            rs_recv.at[b, step * SLABS + slab if step < 2 else 2 * SLABS + step - 2],
            peers[ORDERS[b][slab][step]],
        )

    def reduce_step(b, step):
        rows = pl.ds(0, 2 ** (5 - step) * UNIT)
        return remote(
            (acc2, w2)[b].at[rows, 0:HALF], (got2, got1)[b].at[rows, :],
            rs_send.at[b, step % 2], rs_recv.at[b, 2 * SLABS + max(step, 2) - 2], other_core,
        )

    yh, xh, xq = bits[2], bits[4], bits[5]

    def fold(b, slab, step):
        keep, give, count = ranges(b, slab, step)
        chunk = min(count, 32)

        def total(i):
            here = ours(b, slab, units(keep + i * chunk, chunk))[...]
            return here + theirs(b, slab, units(give + i * chunk, chunk))[...]

        if step == 5:
            full[b, core, yh, xh, xq, :, slab * SLAB : slab * SLAB + SLAB] = total(0)
            return
        for i in range(count // chunk):
            ours(b, slab, units(keep + i * chunk, chunk))[...] = total(i)

    def slabs_of(part):
        return range(8 * part, min(8 * part + 8, SLABS))

    def advance(b, step):
        if step >= 2:
            reduce_step(b, step).wait_recv()
        for slab in range(SLABS):
            if step < 2:
                reduce_copy(b, slab, step, False).wait_recv()
            fold(b, slab, step)
            if step < 5:
                reduce_copy(b, slab, step + 1, True).start()
        reduce_step(b, step).wait_send()

    def begin_reduce(b, part):
        for slab in slabs_of(part):
            reduce_copy(b, slab, 0, True).start()

    for name in ("mid", "s2", "t2", "gp2", "g"):
        for copy in swaps[name]:
            copy.wait_recv()
    for part in range(3):
        weight_products(0, part)
        begin_reduce(0, part)

    def current_tile(j):
        value = dot_nt(gp2[...], w2[broad(j * BROAD), 2 * WIDTH : 4 * WIDTH])
        wide[:, broad(j * BROAD)] = value + g[:, broad(j * BROAD)].astype(f32)

    tiles(2, current_tile)

    def first_backward(c):
        low = c * HALF_ROWS
        rows = slice(low, low + HALF_ROWS)
        tap = tap_in[rows, :].astype(f32)
        total = wide[rows, :] + jnp.where(tx == 3, 0.0, tap)
        gmid[rows, :] = total.astype(bf16)
        swaps["gm"][c].start()

        def slope_tile(j):
            here, there = broad(j * BROAD), broad(WIDTH + j * BROAD)
            grad = dot_nt(gmid[rows, :], q1[here, :])
            gp1[rows, here] = (grad * slope_t[rows, here].astype(f32)).astype(bf16)
            gp1[rows, there] = (grad * slope_g[rows, here].astype(f32)).astype(bf16)

        tiles(2, slope_tile)
        swaps["gp1"][c].start()

    for copy in far_back:
        copy.wait_recv()
    for c in range(HALVES):
        first_backward(c)
    for copy in far_forward + swaps["mid"]:
        copy.wait_send()

    def second_out_tile(j):
        value = dot_nn(t2[...], q2[:, broad(j * BROAD)])
        mid[:, broad(j * BROAD)] = (value + mid[:, broad(j * BROAD)].astype(f32)).astype(bf16)

    tiles(2, second_out_tile)
    store_out = pltpu.make_async_copy(mid, out_frames.at[0], st_sem.at[0])
    store_out.start()
    for name in ("x", "halo", "t1", "gp1", "gm"):
        for copy in swaps[name]:
            copy.wait_recv()
    for part in range(3):
        weight_products(1, part)
        begin_reduce(1, part)
    advance(0, 0)

    for copy in far_back:
        copy.wait_send()

    def first_tap_tile(j):
        value = dot_nt(gp1[...], w1[broad(j * BROAD), 0 : 2 * WIDTH])
        tap_out[:, broad(j * BROAD)] = value.astype(bf16)

    tiles(2, first_tap_tile)
    near_back.start()

    def first_current_tile(j):
        value = dot_nt(gp1[...], w1[broad(j * BROAD), 2 * WIDTH : 4 * WIDTH])
        pre2[:, broad(j * BROAD)] = value + gmid[:, broad(j * BROAD)].astype(f32)

    tiles(2, first_current_tile)
    advance(1, 0)
    advance(0, 1)
    near_back.wait_recv()
    for copy in swaps["gm"]:
        copy.wait_send()
    body_rows = ROWS - NEAR
    gmid[0:body_rows, :] = (
        pre2[0:body_rows, 0:WIDTH] + tap_out[NEAR:ROWS, :].astype(f32)
    ).astype(bf16)
    edge = jnp.where(last_shard, 0.0, near_tap[...].astype(f32))
    gmid[body_rows:ROWS, :] = (pre2[body_rows:ROWS, 0:WIDTH] + edge).astype(bf16)
    store_grad = pltpu.make_async_copy(gmid, frame_grad.at[0], st_sem.at[1])
    store_grad.start()

    left, right = slice(0, HALF // 2), slice(HALF // 2, HALF)

    def gather_copy(b, index, where, target):
        ref = full.at[(b, core) + where]
        return remote(ref, ref, ag_send.at[b, index], ag_recv.at[b, index], target)

    own = (yh, xh, xq)
    beside, below = (yh, xh, 1 - xq), (yh, 1 - xh, xq)
    across, far = (yh, 1 - xh, 1 - xq), (1 - yh, xh, xq)
    far_beside, far_below = (1 - yh, xh, 1 - xq), (1 - yh, 1 - xh, xq)
    far_across = (1 - yh, 1 - xh, 1 - xq)
    moves_out = (
        (own, far_y),
        (own, peers[5]),
        (own, peers[4]),
        (far, peers[5]),
        (far, peers[4]),
        (beside + (every, left), peers[4]),
        (below + (every, right), peers[5]),
        (far_beside + (every, left), peers[4]),
        (far_below + (every, right), peers[5]),
    )

    def gather(b, index):
        return gather_copy(b, index, *moves_out[index])

    def share(b, where):
        return gather_copy(b, 9, where, other_core)

    def stores(b):
        conv, proj = ((conv_total_2, proj_total_2), (conv_total_1, proj_total_1))[b]
        copies = []
        for k in (core, 1 - core):
            moves = (
                (conv, k * 1024, 0, 1024),
                (conv, 2048 + k * 1024, 1024, 1024),
                (proj, k * 512, 2048, 512),
            )
            for target, to, start, width in moves:
                copies.append(
                    pltpu.make_async_copy(
                        full.at[b, k, :, :, :, :, start : start + width],
                        target.at[:, :, :, :, pl.ds(pl.multiple_of(to, width), width)],
                        st_sem.at[2 + b * 6 + len(copies)],
                    )
                )
        return copies

    def gather_stage(b, stage):
        plan = (
            (((), (0, 1, 2), own),),
            (((1,), (5,), beside), ((2,), (6,), below)),
            (((0,), (3, 4), far),),
            (((3,), (7,), far_beside), ((4,), (8,), far_below)),
            (((5, 6), (), across),),
            (((7, 8), (), far_across),),
            (),
        )[stage]
        for waits, starts, piece in plan:
            for index in waits:
                gather(b, index).wait_recv()
            for index in starts:
                gather(b, index).start()
            share(b, piece).start()
        if stage == 6:
            share(b, ()).wait_recv()
        if stage >= 5:
            for copy in stores(b)[3 * stage - 15 : 3 * stage - 12]:
                copy.start()

    for step in range(1, 5):
        advance(1, step)
        advance(0, step + 1)
    gather_stage(0, 0)
    advance(1, 5)
    gather_stage(1, 0)
    for stage in range(1, 6):
        gather_stage(0, stage)
        gather_stage(1, stage)
    near_forward.wait_send()
    near_back.wait_send()
    for name, copies in swaps.items():
        if name not in ("mid", "gm"):
            for copy in copies:
                copy.wait_send()
    store_out.wait()
    store_grad.wait()
    gather_stage(0, 6)
    gather_stage(1, 6)

    for b in range(2):
        for index in range(9):
            gather(b, index).wait_send()
        share(b, ()).wait_send()
        for copy in stores(b):
            copy.wait()


def whole_step(*operands):
    anywhere = pl.BlockSpec(memory_space=pl.ANY)
    bf16, f32 = jnp.bfloat16, jnp.float32
    frame_shape = jax.ShapeDtypeStruct((1, ROWS, WIDTH), bf16)
    totals_shape = (2, 2, 2, 2, 2, UNIT, HALF)
    conv_shape = jax.ShapeDtypeStruct((2, 2, 2, UNIT, 4 * WIDTH), bf16)
    proj_shape = jax.ShapeDtypeStruct((2, 2, 2, UNIT, WIDTH), bf16)
    frame = pltpu.VMEM((ROWS, WIDTH), bf16)
    double = pltpu.VMEM((ROWS, 2 * WIDTH), bf16)
    narrow = pltpu.VMEM((ROWS, WIDTH // 2), bf16)
    weight = pltpu.VMEM((WIDTH, 4 * WIDTH), bf16)
    square = pltpu.VMEM((WIDTH, WIDTH), bf16)
    padded = pltpu.VMEM((ROWS + NEAR, WIDTH), bf16)
    share = pltpu.VMEM((WIDTH, HALF), bf16)
    dma = pltpu.SemaphoreType.DMA
    return pl.pallas_call(
        step_kernel,
        out_shape=[frame_shape, frame_shape] + [conv_shape, proj_shape] * 2,
        in_specs=[anywhere] * 6,
        out_specs=[anywhere] * 6,
        scratch_shapes=[
            weight, weight, square, square,
            padded, frame, frame, frame, frame, frame, frame,
            double, double, frame, frame,
            frame, frame, pltpu.VMEM((NEAR, WIDTH), bf16),
            pltpu.VMEM((ROWS, 2 * WIDTH), f32), pltpu.VMEM((ROWS, WIDTH), f32),
            padded, frame, frame, frame, frame, frame, narrow, frame, narrow,
            share, share, share, pltpu.VMEM(totals_shape, bf16),
            dma((21,)), dma((2,)), dma((2,)), dma((2, CHUNKS)), dma((2, CHUNKS)),
            dma((10, CHUNKS)), dma((10, CHUNKS)),
            dma((2, 2)), dma((2, 2 * SLABS + 4)), dma((2, 10)), dma((2, 10)), dma((14,)),
        ],
        compiler_params=pltpu.CompilerParams(
            collective_id=0, has_side_effects=True, vmem_limit_bytes=67043328
        ),
    )(*operands)


def scaled(total):
    count = lax.axis_size("dp") * lax.axis_size(("tx", "ty")) * ROWS
    value = total.astype(jnp.float32) * float(count) ** (-0.5)
    return value.reshape(128, total.shape[-1])


def shards(*operands):
    block_output, input_gradient, *totals = whole_step(*operands)
    conv_two, proj_two, conv_one, proj_one = (scaled(total) for total in totals)
    return (block_output, input_gradient, conv_one, proj_one, conv_two, proj_two)


def solution(mesh):
    return jax.shard_map(
        shards,
        mesh=mesh,
        in_specs=(P("dp", ("tx", "ty"), None), P(), P(), P(), P(), P("dp", ("tx", "ty"), None)),
        out_specs=(
            P("dp", ("tx", "ty"), None),
            P("dp", ("tx", "ty"), None),
            P("ty", None),
            P("ty", None),
            P("ty", None),
            P("ty", None),
        ),
        check_vma=False,
    )
```
